32 devices in a mesh: scan: 8 (over z, core), det: 4 (over y, x).
Axes of the slice: x: 2, y: 2, z: 4, core: 2. Of those that a mesh axis runs over, the one named last changes fastest.
Arguments:
- patterns: float32 [8, 64, 128, 128], P('scan', None, 'det'), may hold values from -24 to 24, as said below
- encoder_one: float32 [3, 3, 1, 16], replicated, may hold values from -2 to 2
- encoder_two: float32 [3, 3, 16, 32], replicated, may hold values from -0.5 to 0.5
- real_space: float32 [3, 3, 32, 32], replicated, may hold values from -0.375 to 0.375
- decoder_one: float32 [3, 3, 32, 16], replicated, may hold values from -0.5 to 0.5
- decoder_two: float32 [3, 3, 16, 1], replicated, may hold values from -1 to 1
Outputs:
- rebuilt: float32 [8, 64, 128, 128], P('scan', None, 'det')
- misfit: float32 [8, 64], P('scan')
The draws below stay inside these ranges and needn't reach their ends.
Inputs may be any that keep to these rules, and one draw needn't show every extreme that they name: `patterns`: detector intensities after background subtraction, in arbitrary units.
All inputs are finite; a program needn't handle non-finite values.
Results may differ from the reference program's by a relative error of at most 0.00011.
Values sent between devices are 32-bit elements; how exact they have to be, the bound alone decides.
No kernel may reach another device: no remote copies, remote signals or barrier semaphores. Data moves between devices by JAX's collectives and lax.ppermute only.
A program may use at most 128 MiB of HBM per device.

```python
import jax
import jax.numpy as jnp
from jax import lax

DET = 128
F1 = 16
F2 = 32
COLS = 64
NROWS = 8


def draw_patterns(key, part):
    detector = jnp.arange(DET, dtype=jnp.float32)
    row_scale = 0.2 * jnp.exp(jnp.log(10.0) * detector / (DET - 1))
    col_scale = 0.3 * jnp.exp(jnp.log(10.0) * jax.random.uniform(jax.random.fold_in(key, 11), (DET,), jnp.float32))
    scale = row_scale[:, None] * col_scale[None, :]
    value_key = jax.random.fold_in(key, 23)
    values = jnp.clip(jax.random.normal(value_key, (NROWS, COLS, DET, DET), jnp.float32), -4.0, 4.0) * scale
    return values


def bell_draw(own_key, dims, width, most, kind=jnp.bfloat16):
    values = width * jax.random.normal(own_key, dims, jnp.float32)
    return jnp.clip(values, min=-most, max=most).astype(kind)


def setup_inputs(seed: int = 0) -> dict:
    seeds = jax.random.split(jax.random.key(seed), 7)
    return {
        "patterns": draw_patterns(jax.random.fold_in(seeds[6], 71), 0),
        "encoder_one": bell_draw(seeds[1], (3, 3, 1, F1), 9 ** -0.5, 2.0, jnp.float32),
        "encoder_two": bell_draw(seeds[2], (3, 3, F1, F2), (9 * F1) ** -0.5, 0.5, jnp.float32),
        "real_space": bell_draw(seeds[3], (3, 3, F2, F2), (9 * F2) ** -0.5, 0.375, jnp.float32),
        "decoder_one": bell_draw(seeds[4], (3, 3, F2, F1), (9 * F2 // 2) ** -0.5, 0.5, jnp.float32),
        "decoder_two": bell_draw(seeds[5], (3, 3, F1, 1), (9 * F1 // 4) ** -0.5, 1.0, jnp.float32),
    }


def convolve(images, kernel, stride, padding):
    return lax.conv_general_dilated(images, kernel, (stride, stride), padding, dimension_numbers=("NHWC", "HWIO", "NHWC"), precision=lax.Precision.HIGHEST)


def phase_kernel(kernel):
    mapping = jnp.array([[[1.0, 0.0, 0.0], [0.0, 1.0, 1.0], [0.0, 0.0, 0.0]], [[0.0, 0.0, 0.0], [1.0, 1.0, 0.0], [0.0, 0.0, 1.0]]], jnp.float32)
    combined = jnp.einsum("ark,bsl,klio->rsiabo", mapping, mapping, kernel, precision=lax.Precision.HIGHEST)
    return combined.reshape(3, 3, kernel.shape[2], 4 * kernel.shape[3])


def to_space(values, channels):
    shaped = values.reshape(values.shape[0], values.shape[1], values.shape[2], 2, 2, channels)
    shaped = shaped.transpose(0, 1, 3, 2, 4, 5)
    return shaped.reshape(values.shape[0], 2 * values.shape[1], 2 * values.shape[2], channels)


def reference(patterns, encoder_one, encoder_two, real_space, decoder_one, decoder_two):
    both_sides = ((1, 1), (1, 1))

    def encode(row_patterns):
        hidden1 = jax.nn.silu(convolve(row_patterns[..., None], encoder_one, 2, both_sides))
        return jax.nn.silu(convolve(hidden1, encoder_two, 2, both_sides))

    latent = lax.map(encode, patterns)
    padded = jnp.pad(latent, ((1, 1), (1, 1), (0, 0), (0, 0), (0, 0)))
    kernel_one = phase_kernel(decoder_one)
    kernel_two = phase_kernel(decoder_two)

    def finish(row_index):
        window = lax.dynamic_slice_in_dim(padded, row_index, 3, 0)
        summed = jnp.zeros(latent.shape[1:], jnp.float32)
        for row_step in range(3):
            for col_step in range(3):
                summed = summed + jnp.einsum("chwf,fg->chwg", window[row_step, col_step:col_step + COLS], real_space[row_step, col_step], precision=lax.Precision.HIGHEST)
        mixed_map = lax.dynamic_index_in_dim(latent, row_index, 0, keepdims=False) + jax.nn.silu(summed)
        decoded = jax.nn.silu(to_space(convolve(mixed_map, kernel_one, 1, both_sides), F1))
        rebuilt = to_space(convolve(decoded, kernel_two, 1, both_sides), 1)[..., 0]
        target = lax.dynamic_index_in_dim(patterns, row_index, 0, keepdims=False)
        misfit = jnp.mean((rebuilt - target) ** 2, axis=(1, 2))
        return rebuilt, misfit

    rebuilt, misfit = lax.map(finish, jnp.arange(NROWS, dtype=jnp.int32))
    return rebuilt, misfit
```

```python
import functools

import jax
import jax.numpy as jnp
from jax import lax
from jax.experimental import pallas as pl
from jax.experimental.pallas import tpu as pltpu
from jax.sharding import PartitionSpec as P

ABOVE = 7
BELOW = 4
LANES = 128
F32 = jnp.float32
BF16 = jnp.bfloat16


def silu(v):
    return (0.5 * v) * (1.0 + jnp.tanh(0.5 * v))


def split(v):
    high = v.astype(BF16)
    low = (v - high.astype(F32)).astype(BF16)
    return high, low


def iota(shape, dim):
    return lax.broadcasted_iota(jnp.int32, shape, dim)


def spread(values, width):
    k = values.shape[1]
    pick = (iota((k, width), 1) % k == iota((k, width), 0)).astype(F32)
    return jnp.dot(values, pick, precision=lax.Precision.HIGHEST, preferred_element_type=F32)


def put(ref, start, rows, value, lanes=None):
    high, low = split(value)
    third = ref.shape[0] // 3
    lanes = slice(None) if lanes is None else lanes
    ref[start : start + rows, lanes] = high
    ref[third + start : third + start + rows, lanes] = high
    ref[2 * third + start : 2 * third + start + rows, lanes] = low


def stack(block, times):
    return jnp.concatenate([block] * times, axis=0)


ROW_TAPS = {(0, 0): (0, 1), (1, 0): (2,), (0, 1): (0,), (1, 1): (1, 2)}


def weights_body(e1, e2, rs, d1, d2, w1, w2, wm, wd1, wd2):
    f1 = e1.shape[3]
    f2 = e2.shape[3]
    taps = jnp.concatenate([e1[a, b] for a in range(3) for b in range(3)], axis=0)
    wide = spread(taps, w1.shape[1])
    shape = (LANES, w1.shape[1])
    delta = iota(shape, 0) - 2 * (iota(shape, 1) // f1) + 1
    for a in range(3):
        value = jnp.zeros(shape, F32)
        for b in range(3):
            value = jnp.where(delta == b, wide[3 * a + b : 3 * a + b + 1, :], value)
        put(w1, a * LANES, LANES, value)
    shape = (3 * LANES, w2.shape[1])
    delta = iota(shape, 0) // f1 - LANES // f1 - 2 * (iota(shape, 1) // f2) + 1
    for a in range(3):
        value = jnp.zeros(shape, F32)
        for b in range(3):
            value = jnp.where(delta == b, stack(spread(e2[a, b], shape[1]), shape[0] // f1), value)
        put(w2, a * shape[0], shape[0], value)
    odd = lax.axis_index("scan") % 2
    shape = (LANES, LANES)
    same = iota(shape, 0) // f2 == iota(shape, 1) // f2
    for place in range(3):
        for b in range(3):
            if place == 0:
                block = rs[1, b]
            else:
                first = odd == (0 if place == 2 else 1)
                block = jnp.where(first, rs[0, b], rs[2, b])
            value = jnp.where(same, stack(spread(block, LANES), LANES // f2), 0.0)
            put(wm, place * LANES, LANES, value, slice(b * LANES, (b + 1) * LANES))
    per = LANES // f2
    for p in range(2):
        lanes = slice(p * LANES, (p + 1) * LANES)
        w_local = iota(shape, 1) // f1
        k = iota(shape, 0)
        wide_edge = jnp.zeros(shape, F32)
        for r in range(2):
            value = jnp.zeros(shape, F32)
            for b in range(3):
                tap = sum(d1[a, b] for a in ROW_TAPS[r, p])
                tap = stack(spread(tap, LANES), per)
                col = (w_local + b + 1) // 2 - 1
                value = value + jnp.where(col == k // f2, tap, 0.0)
                if r == 0:
                    edge = jnp.where(k // f2 == per - 1, -1, jnp.where(k // f2 == 0, per, -9))
                else:
                    edge = jnp.where(k // f2 == 1, -1, jnp.where(k // f2 == 2, per, -9))
                wide_edge = wide_edge + jnp.where(col == edge, tap, 0.0)
            put(wd1, r * LANES, LANES, value, lanes)
        put(wd1, 2 * LANES, LANES, wide_edge, lanes)
    depth = wd2.shape[0] // 6
    shape = (depth, LANES)
    for p in range(2):
        for r in range(2):
            value = jnp.zeros(shape, F32)
            for b in range(3):
                tap = sum(d2[a, b] for a in ROW_TAPS[r, p])
                tap = stack(jnp.broadcast_to(tap, (f1, LANES)), depth // f1)
                col = (iota(shape, 1) + b + 1) // 2 - 1
                value = value + jnp.where(col == iota(shape, 0) // f1, tap, 0.0)
            put(wd2, r * depth, depth, value, slice(p * LANES, (p + 1) * LANES))


def encode_body(x, halo, w1, w2, out, p0, p1, p2, p3, evh, evl, odh, odl, *, strip, cols):
    rows = strip + ABOVE + BELOW
    parts = (p0, p1, p2, p3)
    for e in range(rows):
        if e < ABOVE:
            value = halo[e]
        elif e < ABOVE + strip:
            value = x[pl.ds(e - ABOVE, cols, stride=strip), :]
        else:
            value = halo[e - strip]
        high, low = split(value)
        m = e // 4
        parts[e % 4][m * cols : (m + 1) * cols, :LANES] = high
        parts[e % 4][m * cols : (m + 1) * cols, LANES:] = low
    n_even = evh.shape[0]
    n_odd = odh.shape[0]
    for ref in (evh, evl, odh, odl):
        ref[:, :LANES] = jnp.zeros((ref.shape[0], LANES), BF16)

    def columns(refs, count):
        high = [ref[start : start + count, :LANES] for ref, start in refs]
        low = [ref[start : start + count, LANES:] for ref, start in refs]
        return jnp.concatenate(high + low + high, axis=1)

    def first(g, carry):
        lanes = pl.ds(pl.multiple_of(g * 256, 256), 256)
        target = pl.ds(pl.multiple_of(LANES + g * 256, LANES), 256)
        for refs, high_ref, low_ref, count in (
            (((p0, 0), (p1, 0), (p2, 0)), evh, evl, n_even),
            (((p2, 0), (p3, 0), (p0, cols)), odh, odl, n_odd),
        ):
            value = silu(jnp.dot(columns(refs, count), w1[:, lanes], preferred_element_type=F32))
            high, low = split(value)
            high_ref[:, target] = high
            low_ref[:, target] = low
        return carry

    lax.fori_loop(0, w1.shape[1] // 256, first, 0)
    n_out = n_odd

    def second(g, carry):
        source = pl.ds(pl.multiple_of(g * 256, 256), 3 * LANES)
        high = [evh[:n_out, source], odh[:, source], evh[cols:, source]]
        low = [evl[:n_out, source], odl[:, source], evl[cols:, source]]
        left = jnp.concatenate(high + low + high, axis=1)
        value = silu(jnp.dot(left, w2[...], preferred_element_type=F32))
        out[:, pl.ds(pl.multiple_of(g * 256, 256), 256)] = value
        return carry

    lax.fori_loop(0, w1.shape[1] // 256, second, 0)


def decode_body(own, sibling, other, x, wm, wd1, wd2, rebuilt, part, mixed, dh, dl, *, strip, cols):
    n = own.shape[0]
    blocks = own.shape[1] // LANES
    rows = n // cols
    det = lax.axis_index("det")
    not_first = (det > 0).astype(F32)
    not_last = (det < lax.axis_size("det") - 1).astype(F32)
    mixed[:, :LANES] = jnp.zeros((n, LANES), F32)
    mixed[:, (blocks + 1) * LANES :] = jnp.zeros((n, LANES), F32)
    position = iota((n, LANES), 0) % cols

    def mix(q, carry):
        lanes = pl.ds(pl.multiple_of(q * LANES, LANES), LANES)
        pairs = [split(ref[:, lanes]) for ref in (own, sibling, other)]
        high = [h for h, _ in pairs]
        low = [v for _, v in pairs]
        left = jnp.concatenate(high + low + high, axis=1)
        y = jnp.dot(left, wm[...], preferred_element_type=F32)
        before = jnp.where(position == 0, 0.0, pltpu.roll(y[:, :LANES], 1, 0))
        after = jnp.where(position == cols - 1, 0.0, pltpu.roll(y[:, 2 * LANES :], n - 1, 0))
        value = own[:, lanes] + silu(y[:, LANES : 2 * LANES] + before + after)
        target = pl.ds(pl.multiple_of((q + 1) * LANES, LANES), LANES)
        mixed[: n - cols, target] = value[: n - cols]
        mixed[n - cols :, target] = value[n - cols :] * not_last
        return carry

    lax.fori_loop(0, blocks, mix, 0)
    count = n - cols
    lane = iota((count, LANES), 1)
    middle = (lane >= 32) & (lane < 96)
    outer = iota((n, LANES), 1) >= 96

    def first(q, carry):
        here = pl.ds(pl.multiple_of((q + 1) * LANES, LANES), LANES)
        before = pl.ds(pl.multiple_of(q * LANES, LANES), LANES)
        after = pl.ds(pl.multiple_of((q + 2) * LANES, LANES), LANES)
        high, low = split(mixed[:, here])
        edges = jnp.where(outer, mixed[:, before], mixed[:, after])
        edges = jnp.where(middle, pltpu.roll(edges[cols:], 64, 1), edges[:count])
        edge_high, edge_low = split(edges)
        highs = [high[:count], high[cols:], edge_high]
        lows = [low[:count], low[cols:], edge_low]
        left = jnp.concatenate(highs + lows + highs, axis=1)
        value = silu(jnp.dot(left, wd1[...], preferred_element_type=F32))
        target = pl.ds(pl.multiple_of(q * LANES, LANES), LANES)
        for i in range(rows - 1):
            for p in range(2):
                block = value[i * cols : (i + 1) * cols, p * LANES : (p + 1) * LANES]
                if i == 0 and p == 0:
                    block = block * not_first
                if i == rows - 2 and p == 1:
                    block = block * not_last
                high, low = split(block)
                start = (2 * i + p) * cols
                dh[start : start + cols, target] = high
                dl[start : start + cols, target] = low
        return carry

    lax.fori_loop(0, blocks, first, 0)
    total = jnp.zeros((cols, LANES), F32)
    pairs = strip // 2 + 1
    step = 6
    for begin in range(0, pairs, step):
        size = min(step, pairs - begin)
        top = slice(begin * cols, (begin + size) * cols)
        bottom = slice((begin + 1) * cols, (begin + size + 1) * cols)
        high = [dh[top], dh[bottom]]
        low = [dl[top], dl[bottom]]
        left = jnp.concatenate(high + low + high, axis=1)
        value = jnp.dot(left, wd2[...], preferred_element_type=F32)
        for i in range(size):
            for p in range(2):
                row = 2 * (begin + i) - 1 + p
                if 0 <= row < strip:
                    block = value[i * cols : (i + 1) * cols, p * LANES : (p + 1) * LANES]
                    where = pl.ds(row, cols, stride=strip)
                    rebuilt[where, :] = block
                    error = block - x[where, :]
                    total = total + error * error
    part[...] = jnp.sum(total.T, axis=0, keepdims=True)


def swapped(value, axis, pairs):
    return lax.ppermute(value, axis, [(i, j) for i, j in pairs] + [(j, i) for i, j in pairs])


def on_device(patterns, encoder_one, encoder_two, real_space, decoder_one, decoder_two):
    _, cols, strip, width = patterns.shape
    f1 = encoder_one.shape[3]
    f2 = encoder_two.shape[3]
    n_scan = lax.axis_size("scan")
    n_det = lax.axis_size("det")
    latent_rows = strip // 4 + 2
    latent_lanes = (width // 4) * f2
    hidden_lanes = (width // 2) * f1
    params = pltpu.CompilerParams(vmem_limit_bytes=56 << 20)
    x = patterns.reshape(cols * strip, width)

    down = [(i, i + 1) for i in range(n_det - 1)]
    up = [(i + 1, i) for i in range(n_det - 1)]
    above = lax.ppermute(patterns[0, :, strip - ABOVE :].transpose(1, 0, 2), "det", down)
    below = lax.ppermute(patterns[0, :, :BELOW].transpose(1, 0, 2), "det", up)
    chips = [(i, i + 1) for i in range(1, n_scan - 1, 2)]
    cores = [(i, i + 1) for i in range(0, n_scan, 2)]
    far_x = swapped(x, "scan", chips)
    halo = jnp.concatenate([above, below], axis=0)
    far_halo = swapped(halo, "scan", chips)

    w1, w2, wm, wd1, wd2 = pl.pallas_call(
        weights_body,
        out_shape=[
            jax.ShapeDtypeStruct((9 * LANES, hidden_lanes), BF16),
            jax.ShapeDtypeStruct((27 * LANES, 256), BF16),
            jax.ShapeDtypeStruct((9 * LANES, 3 * LANES), BF16),
            jax.ShapeDtypeStruct((9 * LANES, 2 * LANES), BF16),
            jax.ShapeDtypeStruct((6 * hidden_lanes, 2 * LANES), BF16),
        ],
        compiler_params=params,
        name="weights",
    )(encoder_one, encoder_two, real_space, decoder_one, decoder_two)

    rows4 = strip // 4 + 3
    n_latent = latent_rows * cols

    def encode(strip_x, strip_halo):
        return pl.pallas_call(
            functools.partial(encode_body, strip=strip, cols=cols),
            out_shape=jax.ShapeDtypeStruct((n_latent, latent_lanes), F32),
            scratch_shapes=[pltpu.VMEM((rows4 * cols, 2 * LANES), BF16)] * 4
            + [pltpu.VMEM((n_latent + cols, hidden_lanes + LANES), BF16)] * 2
            + [pltpu.VMEM((n_latent, hidden_lanes + LANES), BF16)] * 2,
            compiler_params=params,
            name="encode",
        )(strip_x, strip_halo, w1, w2)

    own = encode(x, halo)
    sibling = swapped(own, "scan", cores)
    other = encode(far_x, far_halo)
    rebuilt, part = pl.pallas_call(
        functools.partial(decode_body, strip=strip, cols=cols),
        out_shape=[
            jax.ShapeDtypeStruct((cols * strip, width), F32),
            jax.ShapeDtypeStruct((1, cols), F32),
        ],
        scratch_shapes=[
            pltpu.VMEM((n_latent, latent_lanes + 2 * LANES), F32),
            pltpu.VMEM(((strip // 2 + 2) * cols, hidden_lanes), BF16),
            pltpu.VMEM(((strip // 2 + 2) * cols, hidden_lanes), BF16),
        ],
        compiler_params=params,
        name="decode",
    )(own, sibling, other, x, wm, wd1, wd2)
    misfit = lax.psum(part, "det") / (width * width)
    return rebuilt.reshape(patterns.shape), misfit


def solution(mesh):
    return jax.shard_map(
        on_device,
        mesh=mesh,
        in_specs=(P("scan", None, "det", None), P(), P(), P(), P(), P()),
        out_specs=(P("scan", None, "det", None), P("scan", None)),
        check_vma=False,
    )
```

```python
import functools

import jax
import jax.numpy as jnp
from jax import lax
from jax.experimental import pallas as pl
from jax.experimental.pallas import tpu as pltpu
from jax.sharding import PartitionSpec as P

ABOVE = 7
BELOW = 4
LANES = 128
F32 = jnp.float32
BF16 = jnp.bfloat16
ENCODE_VMEM = 28 << 20
DECODE_VMEM = 36 << 20


def silu(v):
    return (0.5 * v) * (1.0 + jnp.tanh(0.5 * v))


def split(v):
    high = v.astype(BF16)
    low = (v - high.astype(F32)).astype(BF16)
    return high, low


def iota(shape, dim):
    return lax.broadcasted_iota(jnp.int32, shape, dim)


def spread(values, width):
    k = values.shape[1]
    pick = (iota((k, width), 1) % k == iota((k, width), 0)).astype(F32)
    return jnp.dot(values, pick, precision=lax.Precision.HIGHEST, preferred_element_type=F32)


def put(ref, start, value, lanes=None):
    high, low = split(value)
    half = ref.shape[0] // 2
    rows = value.shape[0]
    lanes = slice(None) if lanes is None else lanes
    ref[start : start + rows, lanes] = high
    ref[half + start : half + start + rows, lanes] = low


def thrice(ref):
    half = ref.shape[0] // 2
    return jnp.concatenate([ref[:half], ref[:half], ref[half:]], axis=0)


def stack(block, times):
    return jnp.concatenate([block] * times, axis=0)


def mosaic(refs):
    return jnp.concatenate([refs[a, b] for a in range(3) for b in range(3)], axis=0)


TAPS = 42
ROW_TAPS = {(0, 0): (0, 1), (1, 0): (2,), (0, 1): (0,), (1, 1): (1, 2)}


def encoder_weights_body(e1, e2, w1, w2):
    f1 = e1.shape[3]
    f2 = e2.shape[3]
    wide = spread(mosaic(e1), w1.shape[1])
    shape = (LANES, w1.shape[1])
    k = iota(shape, 0)
    n = iota(shape, 1)
    group = n // 256
    place = (k - 32 * group + 1) & (LANES - 1)
    a = (place >= TAPS).astype(jnp.int32) + (place >= 2 * TAPS).astype(jnp.int32)
    col = place - TAPS * a
    b = col - 2 * ((n // f1) % (256 // f1))
    good = (b >= 0) & (b <= 2) & ((group > 0) | (col > 0))
    key = jnp.where(good, 3 * a + b, -1)
    value = jnp.zeros(shape, F32)
    for tap in range(9):
        value = jnp.where(key == tap, wide[tap : tap + 1, :], value)
    put(w1, 0, value)
    wide = spread(mosaic(e2), w2.shape[1])
    shape = (3 * LANES, w2.shape[1])
    delta = iota(shape, 0) // f1 - LANES // f1 - 2 * (iota(shape, 1) // f2) + 1
    for a in range(3):
        value = jnp.zeros(shape, F32)
        for b in range(3):
            tap = wide[(3 * a + b) * f1 : (3 * a + b + 1) * f1]
            value = jnp.where(delta == b, stack(tap, shape[0] // f1), value)
        put(w2, a * shape[0], value)


def decoder_weights_body(rs, d1, d2, wm, wd1, wd2):
    f2, f1 = d1.shape[3], d1.shape[2]
    odd = lax.axis_index("scan") % 2
    shape = (LANES, LANES)
    same = iota(shape, 0) // f2 == iota(shape, 1) // f2
    wide = spread(mosaic(rs), LANES)
    tap = {(a, b): wide[(3 * a + b) * f2 : (3 * a + b + 1) * f2] for a in range(3) for b in range(3)}
    for place in range(3):
        for b in range(3):
            if place == 0:
                block = tap[1, b]
            else:
                block = jnp.where(odd == (0 if place == 2 else 1), tap[0, b], tap[2, b])
            value = jnp.where(same, stack(block, LANES // f2), 0.0)
            put(wm, place * LANES, value, slice(b * LANES, (b + 1) * LANES))
    per = LANES // f2
    wide = spread(jnp.concatenate([d1[a, b].T for a in range(3) for b in range(3)], axis=0), LANES)
    tap = {(a, b): wide[(3 * a + b) * f2 : (3 * a + b + 1) * f2] for a in range(3) for b in range(3)}
    w_local = iota(shape, 1) // f1
    k = iota(shape, 0)
    for p in range(2):
        lanes = slice(p * LANES, (p + 1) * LANES)
        wide_edge = jnp.zeros(shape, F32)
        for r in range(2):
            value = jnp.zeros(shape, F32)
            for b in range(3):
                block = stack(sum(tap[a, b] for a in ROW_TAPS[r, p]), per)
                col = (w_local + b + 1) // 2 - 1
                value = value + jnp.where(col == k // f2, block, 0.0)
                if r == 0:
                    edge = jnp.where(k // f2 == per - 1, -1, jnp.where(k // f2 == 0, per, -9))
                else:
                    edge = jnp.where(k // f2 == 1, -1, jnp.where(k // f2 == 2, per, -9))
                wide_edge = wide_edge + jnp.where(col == edge, block, 0.0)
            put(wd1, r * LANES, value, lanes)
        put(wd1, 2 * LANES, wide_edge, lanes)
    depth = wd2.shape[0] // 4
    shape = (depth, LANES)
    diagonal = iota((f1, f1), 0) == iota((f1, f1), 1)
    column = {
        (a, b): jnp.sum(jnp.where(diagonal, d2[a, b], 0.0), axis=1, keepdims=True)
        for a in range(3)
        for b in range(3)
    }
    for p in range(2):
        for r in range(2):
            value = jnp.zeros(shape, F32)
            for b in range(3):
                block = jnp.broadcast_to(sum(column[a, b] for a in ROW_TAPS[r, p]), (f1, LANES))
                col = (iota(shape, 1) + b + 1) // 2 - 1
                value = value + jnp.where(col == iota(shape, 0) // f1, stack(block, depth // f1), 0.0)
            put(wd2, r * depth, value, slice(p * LANES, (p + 1) * LANES))


def encode_body(x, halo, w1, w2, out, tap0, tap1, tap2, high_map, low_map, *, strip, cols):
    rows = strip + ABOVE + BELOW
    n_odd = strip // 4 + 2
    n_even = n_odd + 1
    odd_start = n_even * cols

    def place(h):
        start = (h // 2) * cols + (h % 2) * odd_start
        return slice(start, start + cols)

    for e in range(rows):
        if e < ABOVE:
            value = halo[e]
        elif e < ABOVE + strip:
            value = x[pl.ds(e - ABOVE, cols, stride=strip), :]
        else:
            value = halo[e - strip]
        if e % 2:
            tap1[place(e // 2), :] = pltpu.roll(value, TAPS, 1)
        else:
            if e // 2 < n_even + n_odd:
                tap0[place(e // 2), :] = value
            if e > 0:
                tap2[place(e // 2 - 1), :] = pltpu.roll(value, 2 * TAPS, 1)
    total = high_map.shape[0]
    for ref in (high_map, low_map):
        ref[:, :LANES] = jnp.zeros((total, LANES), BF16)
    lane = iota((total, LANES), 1)

    def first(g, carry):
        lanes = pl.ds(pl.multiple_of(g * 256, 256), 256)
        target = pl.ds(pl.multiple_of(LANES + g * 256, LANES), 256)
        at = (lane - 32 * g + 1) & (LANES - 1)
        packed = jnp.where(at < TAPS, tap0[...], jnp.where(at < 2 * TAPS, tap1[...], tap2[...]))
        high, low = split(packed)
        left = jnp.concatenate([high, low, high], axis=1)
        value = silu(jnp.dot(left, thrice(w1.at[:, lanes]), preferred_element_type=F32))
        high, low = split(value)
        high_map[:, target] = high
        low_map[:, target] = low
        return carry

    groups = (high_map.shape[1] - LANES) // 256
    lax.fori_loop(0, groups, first, 0)
    n = n_odd * cols

    def second(g, carry):
        source = pl.ds(pl.multiple_of(g * 256, 256), 3 * LANES)
        starts = (0, odd_start, cols)
        high = [high_map[start : start + n, source] for start in starts]
        low = [low_map[start : start + n, source] for start in starts]
        left = jnp.concatenate(high + low + high, axis=1)
        value = silu(jnp.dot(left, thrice(w2), preferred_element_type=F32))
        out[:, pl.ds(pl.multiple_of(g * 256, 256), 256)] = value
        return carry

    lax.fori_loop(0, groups, second, 0)


def decode_body(own, sibling, other, x, wm, wd1, wd2, rebuilt, part, mixed, dh, dl, *, strip, cols):
    n = own.shape[0]
    blocks = own.shape[1] // LANES
    rows = n // cols
    det = lax.axis_index("det")
    not_first = (det > 0).astype(F32)
    not_last = (det < lax.axis_size("det") - 1).astype(F32)
    mixed[:, :LANES] = jnp.zeros((n, LANES), F32)
    mixed[:, (blocks + 1) * LANES :] = jnp.zeros((n, LANES), F32)
    position = iota((n, LANES), 0) % cols

    def mix(q, carry):
        lanes = pl.ds(pl.multiple_of(q * LANES, LANES), LANES)
        pairs = [split(ref[:, lanes]) for ref in (own, sibling, other)]
        high = [h for h, _ in pairs]
        low = [v for _, v in pairs]
        left = jnp.concatenate(high + low + high, axis=1)
        y = jnp.dot(left, thrice(wm), preferred_element_type=F32)
        before = jnp.where(position == 0, 0.0, pltpu.roll(y[:, :LANES], 1, 0))
        after = jnp.where(position == cols - 1, 0.0, pltpu.roll(y[:, 2 * LANES :], n - 1, 0))
        value = own[:, lanes] + silu(y[:, LANES : 2 * LANES] + before + after)
        target = pl.ds(pl.multiple_of((q + 1) * LANES, LANES), LANES)
        mixed[: n - cols, target] = value[: n - cols]
        mixed[n - cols :, target] = value[n - cols :] * not_last
        return carry

    lax.fori_loop(0, blocks, mix, 0)
    count = n - cols
    lane = iota((count, LANES), 1)
    middle = (lane >= 32) & (lane < 96)
    outer = iota((n, LANES), 1) >= 96

    def first(q, carry):
        here = pl.ds(pl.multiple_of((q + 1) * LANES, LANES), LANES)
        before = pl.ds(pl.multiple_of(q * LANES, LANES), LANES)
        after = pl.ds(pl.multiple_of((q + 2) * LANES, LANES), LANES)
        high, low = split(mixed[:, here])
        edges = jnp.where(outer, mixed[:, before], mixed[:, after])
        edges = jnp.where(middle, pltpu.roll(edges[cols:], 64, 1), edges[:count])
        edge_high, edge_low = split(edges)
        highs = [high[:count], high[cols:], edge_high]
        lows = [low[:count], low[cols:], edge_low]
        left = jnp.concatenate(highs + lows + highs, axis=1)
        value = silu(jnp.dot(left, thrice(wd1), preferred_element_type=F32))
        target = pl.ds(pl.multiple_of(q * LANES, LANES), LANES)
        for i in range(rows - 1):
            for p in range(2):
                block = value[i * cols : (i + 1) * cols, p * LANES : (p + 1) * LANES]
                if i == 0 and p == 0:
                    block = block * not_first
                if i == rows - 2 and p == 1:
                    block = block * not_last
                high, low = split(block)
                start = (2 * i + p) * cols
                dh[start : start + cols, target] = high
                dl[start : start + cols, target] = low
        return carry

    lax.fori_loop(0, blocks, first, 0)
    total = jnp.zeros((cols, LANES), F32)
    pairs = strip // 2 + 1
    step = 6
    for begin in range(0, pairs, step):
        size = min(step, pairs - begin)
        top = slice(begin * cols, (begin + size) * cols)
        bottom = slice((begin + 1) * cols, (begin + size + 1) * cols)
        high = [dh[top], dh[bottom]]
        low = [dl[top], dl[bottom]]
        left = jnp.concatenate(high + low + high, axis=1)
        value = jnp.dot(left, thrice(wd2), preferred_element_type=F32)
        for i in range(size):
            for p in range(2):
                row = 2 * (begin + i) - 1 + p
                if 0 <= row < strip:
                    block = value[i * cols : (i + 1) * cols, p * LANES : (p + 1) * LANES]
                    where = pl.ds(row, cols, stride=strip)
                    rebuilt[where, :] = block
                    error = block - x[where, :]
                    total = total + error * error
    part[...] = jnp.sum(total.T, axis=0, keepdims=True) * (1.0 / (LANES * LANES))


def swapped(value, axis, pairs):
    return lax.ppermute(value, axis, [(i, j) for i, j in pairs] + [(j, i) for i, j in pairs])


def on_device(patterns, encoder_one, encoder_two, real_space, decoder_one, decoder_two):
    _, cols, strip, width = patterns.shape
    f1 = encoder_one.shape[3]
    f2 = encoder_two.shape[3]
    n_scan = lax.axis_size("scan")
    n_det = lax.axis_size("det")
    latent_rows = strip // 4 + 2
    latent_lanes = (width // 4) * f2
    hidden_lanes = (width // 2) * f1
    x = patterns.reshape(cols * strip, width)

    down = [(i, i + 1) for i in range(n_det - 1)]
    up = [(i + 1, i) for i in range(n_det - 1)]
    above = lax.ppermute(patterns[0, :, strip - ABOVE :].transpose(1, 0, 2), "det", down)
    below = lax.ppermute(patterns[0, :, :BELOW].transpose(1, 0, 2), "det", up)
    chips = [(i, i + 1) for i in range(1, n_scan - 1, 2)]
    cores = [(i, i + 1) for i in range(0, n_scan, 2)]
    far_x = swapped(x, "scan", chips)
    halo = jnp.concatenate([above, below], axis=0)
    far_halo = swapped(halo, "scan", chips)

    def cost(flops, moved):
        return pl.CostEstimate(flops=flops, transcendentals=0, bytes_accessed=moved)

    w1, w2 = pl.pallas_call(
        encoder_weights_body,
        out_shape=[
            jax.ShapeDtypeStruct((2 * LANES, hidden_lanes), BF16),
            jax.ShapeDtypeStruct((18 * LANES, 256), BF16),
        ],
        compiler_params=pltpu.CompilerParams(vmem_limit_bytes=12 << 20),
        cost_estimate=cost(10**9, 2 << 20),
        name="encoder_weights",
    )(encoder_one, encoder_two)
    wm, wd1, wd2 = pl.pallas_call(
        decoder_weights_body,
        out_shape=[
            jax.ShapeDtypeStruct((6 * LANES, 3 * LANES), BF16),
            jax.ShapeDtypeStruct((6 * LANES, 2 * LANES), BF16),
            jax.ShapeDtypeStruct((4 * hidden_lanes, 2 * LANES), BF16),
        ],
        compiler_params=pltpu.CompilerParams(vmem_limit_bytes=12 << 20),
        cost_estimate=cost(10**9, 4 << 20),
        name="decoder_weights",
    )(real_space, decoder_one.transpose(0, 1, 3, 2), decoder_two.transpose(0, 1, 3, 2))

    n_latent = latent_rows * cols
    n_hidden = (2 * latent_rows + 1) * cols

    def encode(strip_x, strip_halo):
        return pl.pallas_call(
            functools.partial(encode_body, strip=strip, cols=cols),
            out_shape=jax.ShapeDtypeStruct((n_latent, latent_lanes), F32),
            scratch_shapes=[pltpu.VMEM((n_hidden, LANES), F32)] * 3
            + [pltpu.VMEM((n_hidden, hidden_lanes + LANES), BF16)] * 2,
            compiler_params=pltpu.CompilerParams(vmem_limit_bytes=ENCODE_VMEM),
            cost_estimate=cost(2 * n_latent * 27 * LANES * latent_lanes * 8, 8 << 20),
            name="encode",
        )(strip_x, strip_halo, w1, w2)

    own = encode(x, halo)
    sibling = swapped(own, "scan", cores)
    other = encode(far_x, far_halo)
    rebuilt, part = pl.pallas_call(
        functools.partial(decode_body, strip=strip, cols=cols),
        out_shape=[
            jax.ShapeDtypeStruct((cols * strip, width), F32),
            jax.ShapeDtypeStruct((1, cols), F32),
        ],
        scratch_shapes=[
            pltpu.VMEM((n_latent, latent_lanes + 2 * LANES), F32),
            pltpu.VMEM(((strip // 2 + 2) * cols, hidden_lanes), BF16),
            pltpu.VMEM(((strip // 2 + 2) * cols, hidden_lanes), BF16),
        ],
        compiler_params=pltpu.CompilerParams(vmem_limit_bytes=DECODE_VMEM),
        cost_estimate=cost(2 * n_latent * 45 * LANES * latent_lanes, 16 << 20),
        name="decode",
    )(own, sibling, other, x, wm, wd1, wd2)
    if n_det == 4:
        misfit = part
        for turn in range(1, n_det):
            misfit = misfit + lax.ppermute(part, "det", [(i, (i + turn) % n_det) for i in range(n_det)])
    else:
        misfit = lax.psum(part, "det")
    return rebuilt.reshape(patterns.shape), misfit


def solution(mesh):
    return jax.shard_map(
        on_device,
        mesh=mesh,
        in_specs=(P("scan", None, "det", None), P(), P(), P(), P(), P()),
        out_specs=(P("scan", None, "det", None), P("scan", None)),
        check_vma=False,
    )
```

```python
import functools

import jax
import jax.numpy as jnp
from jax import lax
from jax.experimental import pallas as pl
from jax.experimental.pallas import tpu as pltpu
from jax.sharding import PartitionSpec as P

ABOVE = 7
BELOW = 4
LANES = 128
F32 = jnp.float32
BF16 = jnp.bfloat16
ENCODE_VMEM = 28 << 20
DECODE_VMEM = 36 << 20


def silu(v):
    return (0.5 * v) * (1.0 + jnp.tanh(0.5 * v))


def split(v):
    high = v.astype(BF16)
    low = (v - high.astype(F32)).astype(BF16)
    return high, low


def iota(shape, dim):
    return lax.broadcasted_iota(jnp.int32, shape, dim)


def spread(values, width):
    k = values.shape[1]
    pick = (iota((k, width), 1) % k == iota((k, width), 0)).astype(F32)
    return jnp.dot(values, pick, precision=lax.Precision.HIGHEST, preferred_element_type=F32)


def put(ref, start, value, lanes=None):
    high, low = split(value)
    half = ref.shape[0] // 2
    rows = value.shape[0]
    lanes = slice(None) if lanes is None else lanes
    ref[start : start + rows, lanes] = high
    ref[half + start : half + start + rows, lanes] = low


def thrice(ref):
    half = ref.shape[0] // 2
    return jnp.concatenate([ref[:half], ref[:half], ref[half:]], axis=0)


def stack(block, times):
    return jnp.concatenate([block] * times, axis=0)


def mosaic(refs):
    return jnp.concatenate([refs[a, b] for a in range(3) for b in range(3)], axis=0)


TAPS = 42
ROW_TAPS = {(0, 0): (0, 1), (1, 0): (2,), (0, 1): (0,), (1, 1): (1, 2)}


def own_lane(shape):
    return iota(shape, len(shape) - 1) ^ (lax.axis_index("scan") % 2 * (LANES // 2))


def weights_body(*refs):
    sources, outputs, targets, sems = refs[:5], refs[5:10], refs[10:15], refs[15]
    copies = [pltpu.make_async_copy(a, b, sems.at[i]) for i, (a, b) in enumerate(zip(sources, targets))]
    for copy in copies:
        copy.start()
    for copy in copies:
        copy.wait()
    e1, e2, rs, d1, d2 = targets
    w1, w2, wm, wd1, wd2 = outputs
    encoder_weights(e1, e2, w1, w2)
    decoder_weights(rs, d1, d2, wm, wd1, wd2)


def encoder_weights(e1, e2, w1, w2):
    f1 = e1.shape[3]
    f2 = e2.shape[3]
    wide = spread(mosaic(e1), w1.shape[1])
    shape = (LANES, w1.shape[1])
    k = iota(shape, 0)
    n = iota(shape, 1)
    group = n // 256
    place = (k - 32 * group + 1) & (LANES - 1)
    a = (place >= TAPS).astype(jnp.int32) + (place >= 2 * TAPS).astype(jnp.int32)
    col = place - TAPS * a
    b = col - 2 * ((n // f1) % (256 // f1))
    good = (b >= 0) & (b <= 2) & ((group > 0) | (col > 0))
    key = jnp.where(good, 3 * a + b, -1)
    value = jnp.zeros(shape, F32)
    for tap in range(9):
        value = jnp.where(key == tap, wide[tap : tap + 1, :], value)
    put(w1, 0, value)
    wide = spread(mosaic(e2), w2.shape[1])
    shape = (256, w2.shape[1])
    out_col = own_lane(shape) // f2
    delta = iota(shape, 0) // f1 - 2 * out_col + 1
    for a in range(3):
        value = jnp.zeros(shape, F32)
        for b in range(3):
            tap = wide[(3 * a + b) * f1 : (3 * a + b + 1) * f1]
            value = jnp.where(delta == b, stack(tap, shape[0] // f1), value)
        put(w2, a * shape[0], value)
    shape = (LANES, w2.shape[1])
    slot = iota(shape, 0) // f1
    value = jnp.zeros(shape, F32)
    for a, at in enumerate((LANES // f1 - 1, 0, 1)):
        tap = stack(wide[3 * a * f1 : (3 * a + 1) * f1], LANES // f1)
        value = jnp.where((slot == at) & (own_lane(shape) // f2 == 0), tap, value)
    put(w2, 3 * 256, value)


def decoder_weights(rs, d1, d2, wm, wd1, wd2):
    f2, f1 = d1.shape[3], d1.shape[2]
    odd = lax.axis_index("scan") % 2
    shape = (LANES, LANES)
    wide = spread(mosaic(rs), LANES)

    def tap(a, b):
        return stack(wide[(3 * a + b) * f2 : (3 * a + b + 1) * f2], LANES // f2)

    def outer(first, b):
        return jnp.where(odd == first, tap(0, b), tap(2, b))

    k = iota(shape, 0) ^ (odd * (LANES // 2))
    n = own_lane(shape)
    same = (k // f2) % 2 == (n // f2) % 2
    for half in range(2):
        row_here = k // (LANES // 2) == half
        col_here = n // (LANES // 2) == half
        for part in range(2):
            if part == 0:
                block = [jnp.where(row_here, tap(1, b), outer(1, b)) for b in range(3)]
                good = same
            else:
                block = [outer(0, b) for b in range(3)]
                good = same & row_here
            sides = jnp.where(good, jnp.where(col_here, block[0], block[2]), 0.0)
            centre = jnp.where(good & col_here, block[1], 0.0)
            put(wm, part * LANES, sides, slice(half * 256, half * 256 + LANES))
            put(wm, part * LANES, centre, slice(half * 256 + LANES, half * 256 + 256))
    per = LANES // f2
    wide = spread(jnp.concatenate([d1[a, b].T for a in range(3) for b in range(3)], axis=0), LANES)
    tap = {(a, b): wide[(3 * a + b) * f2 : (3 * a + b + 1) * f2] for a in range(3) for b in range(3)}
    w_local = iota(shape, 1) // f1
    for p in range(2):
        lanes = slice(p * LANES, (p + 1) * LANES)
        wide_edge = jnp.zeros(shape, F32)
        for r in range(2):
            value = jnp.zeros(shape, F32)
            for b in range(3):
                block = stack(sum(tap[a, b] for a in ROW_TAPS[r, p]), per)
                col = (w_local + b + 1) // 2 - 1
                value = value + jnp.where(col == k // f2, block, 0.0)
                if r == 0:
                    edge = jnp.where(k // f2 == per - 1, -1, jnp.where(k // f2 == 0, per, -9))
                else:
                    edge = jnp.where(k // f2 == 1, -1, jnp.where(k // f2 == 2, per, -9))
                wide_edge = wide_edge + jnp.where(col == edge, block, 0.0)
            put(wd1, r * LANES, value, lanes)
        put(wd1, 2 * LANES, wide_edge, lanes)
    depth = wd2.shape[0] // 4
    shape = (depth, LANES)
    diagonal = iota((f1, f1), 0) == iota((f1, f1), 1)
    column = {
        (a, b): jnp.sum(jnp.where(diagonal, d2[a, b], 0.0), axis=1, keepdims=True)
        for a in range(3)
        for b in range(3)
    }
    for p in range(2):
        for r in range(2):
            value = jnp.zeros(shape, F32)
            for b in range(3):
                block = jnp.broadcast_to(sum(column[a, b] for a in ROW_TAPS[r, p]), (f1, LANES))
                col = (iota(shape, 1) + b + 1) // 2 - 1
                value = value + jnp.where(col == iota(shape, 0) // f1, stack(block, depth // f1), 0.0)
            put(wd2, r * depth, value, slice(p * LANES, (p + 1) * LANES))


def encode_body(
    x, halo, w1, w2, out, tap0, tap1, tap2, high_map, low_map, high_edge, low_edge, *, strip, cols, step
):
    rows = strip + ABOVE + BELOW
    n_odd = strip // 4 + 2
    n_even = n_odd + 1
    odd_start = n_even * cols

    def place(h):
        start = (h // 2) * cols + (h % 2) * odd_start
        return slice(start, start + cols)

    for e in range(rows):
        if e < ABOVE:
            value = halo[e]
        elif e < ABOVE + strip:
            value = x[pl.ds(e - ABOVE, cols, stride=strip), :]
        else:
            value = halo[e - strip]
        if e % 2:
            tap1[place(e // 2), :] = pltpu.roll(value, TAPS, 1)
        else:
            if e // 2 < n_even + n_odd:
                tap0[place(e // 2), :] = value
            if e > 0:
                tap2[place(e // 2 - 1), :] = pltpu.roll(value, 2 * TAPS, 1)
    total = high_map.shape[0]
    n = n_odd * cols
    for ref in (high_edge, low_edge):
        ref[:, :LANES] = jnp.zeros((n, LANES), BF16)
    lane = iota((total, LANES), 1)
    edge_lane = iota((n, LANES), 1)
    groups = high_map.shape[1] // 256

    def first(g, carry):
        lanes = pl.ds(pl.multiple_of(g * 256, 256), 256)
        at = (lane - 32 * g + 1) & (LANES - 1)
        packed = jnp.where(at < TAPS, tap0[...], jnp.where(at < 2 * TAPS, tap1[...], tap2[...]))
        high, low = split(packed)
        left = jnp.concatenate([high, low, high], axis=1)
        value = silu(jnp.dot(left, thrice(w1.at[:, lanes]), preferred_element_type=F32))
        high, low = split(value)
        high_map[:, lanes] = high
        low_map[:, lanes] = low
        last = value[:, LANES:]
        one = pltpu.roll(last[odd_start:], step, 1)
        two = pltpu.roll(last[cols:odd_start], 2 * step, 1)
        edge = jnp.where(edge_lane < step, one, jnp.where(edge_lane < 2 * step, two, last[:n]))
        high, low = split(edge)
        target = pl.ds(pl.multiple_of((g + 1) * LANES, LANES), LANES)
        high_edge[:, target] = high
        low_edge[:, target] = low
        return carry

    lax.fori_loop(0, groups, first, 0)

    def second(g, carry):
        source = pl.ds(pl.multiple_of(g * 256, 256), 256)
        beside = pl.ds(pl.multiple_of(g * LANES, LANES), LANES)
        starts = (0, odd_start, cols)
        high = [high_map[start : start + n, source] for start in starts] + [high_edge[:, beside]]
        low = [low_map[start : start + n, source] for start in starts] + [low_edge[:, beside]]
        left = jnp.concatenate(high + low + high, axis=1)
        out[:, source] = silu(jnp.dot(left, thrice(w2), preferred_element_type=F32))
        return carry

    lax.fori_loop(0, groups, second, 0)


def decode_body(own, sibling, other, x, wm, wd1, wd2, rebuilt, part, mixed, dh, dl, *, strip, cols):
    n = own.shape[0]
    blocks = own.shape[1] // LANES
    rows = n // cols
    det = lax.axis_index("det")
    not_first = (det > 0).astype(F32)
    not_last = (det < lax.axis_size("det") - 1).astype(F32)
    mixed[:, :LANES] = jnp.zeros((n, LANES), F32)
    mixed[:, (blocks + 1) * LANES :] = jnp.zeros((n, LANES), F32)
    position = iota((n, LANES), 0) % cols
    below = own_lane((n, LANES)) < LANES // 2

    def mix(q, carry):
        lanes = pl.ds(pl.multiple_of(q * LANES, LANES), LANES)
        mine, beside = own[:, lanes], sibling[:, lanes]
        other_high, other_low = split(other[:, lanes])
        sides, centres = [], []
        for half, joined in enumerate((jnp.where(below, mine, beside), jnp.where(below, beside, mine))):
            high, low = split(joined)
            left = jnp.concatenate([high, other_high, low, other_low, high, other_high], axis=1)
            y = jnp.dot(left, thrice(wm.at[:, half * 256 : half * 256 + 256]), preferred_element_type=F32)
            sides.append(y[:, :LANES])
            centres.append(y[:, LANES:])
        before = pltpu.roll(jnp.where(below, sides[0], sides[1]), 1, 0)
        after = pltpu.roll(pltpu.roll(jnp.where(below, sides[1], sides[0]), LANES // 2, 1), n - 1, 0)
        before = jnp.where(position == 0, 0.0, before)
        after = jnp.where(position == cols - 1, 0.0, after)
        value = mine + silu(centres[0] + centres[1] + before + after)
        target = pl.ds(pl.multiple_of((q + 1) * LANES, LANES), LANES)
        mixed[: n - cols, target] = value[: n - cols]
        mixed[n - cols :, target] = value[n - cols :] * not_last
        return carry

    lax.fori_loop(0, blocks, mix, 0)
    count = n - cols
    lane = own_lane((count, LANES))
    middle = (lane >= 32) & (lane < 96)
    outer = own_lane((n, LANES)) >= 96

    def first(q, carry):
        here = pl.ds(pl.multiple_of((q + 1) * LANES, LANES), LANES)
        before = pl.ds(pl.multiple_of(q * LANES, LANES), LANES)
        after = pl.ds(pl.multiple_of((q + 2) * LANES, LANES), LANES)
        high, low = split(mixed[:, here])
        edges = jnp.where(outer, mixed[:, before], mixed[:, after])
        edges = jnp.where(middle, pltpu.roll(edges[cols:], 64, 1), edges[:count])
        edge_high, edge_low = split(edges)
        highs = [high[:count], high[cols:], edge_high]
        lows = [low[:count], low[cols:], edge_low]
        left = jnp.concatenate(highs + lows + highs, axis=1)
        value = silu(jnp.dot(left, thrice(wd1), preferred_element_type=F32))
        target = pl.ds(pl.multiple_of(q * LANES, LANES), LANES)
        for i in range(rows - 1):
            for p in range(2):
                block = value[i * cols : (i + 1) * cols, p * LANES : (p + 1) * LANES]
                if i == 0 and p == 0:
                    block = block * not_first
                if i == rows - 2 and p == 1:
                    block = block * not_last
                high, low = split(block)
                start = (2 * i + p) * cols
                dh[start : start + cols, target] = high
                dl[start : start + cols, target] = low
        return carry

    lax.fori_loop(0, blocks, first, 0)
    total = jnp.zeros((cols, LANES), F32)
    pairs = strip // 2 + 1
    step = 6
    for begin in range(0, pairs, step):
        size = min(step, pairs - begin)
        top = slice(begin * cols, (begin + size) * cols)
        bottom = slice((begin + 1) * cols, (begin + size + 1) * cols)
        high = [dh[top], dh[bottom]]
        low = [dl[top], dl[bottom]]
        left = jnp.concatenate(high + low + high, axis=1)
        value = jnp.dot(left, thrice(wd2), preferred_element_type=F32)
        for i in range(size):
            for p in range(2):
                row = 2 * (begin + i) - 1 + p
                if 0 <= row < strip:
                    block = value[i * cols : (i + 1) * cols, p * LANES : (p + 1) * LANES]
                    where = pl.ds(row, cols, stride=strip)
                    rebuilt[where, :] = block
                    error = block - x[where, :]
                    total = total + error * error
    part[...] = jnp.sum(total.T, axis=0, keepdims=True) * (1.0 / (LANES * LANES))


def swapped(value, axis, pairs):
    return lax.ppermute(value, axis, [(i, j) for i, j in pairs] + [(j, i) for i, j in pairs])


def on_device(patterns, encoder_one, encoder_two, real_space, decoder_one, decoder_two):
    _, cols, strip, width = patterns.shape
    f1 = encoder_one.shape[3]
    f2 = encoder_two.shape[3]
    n_scan = lax.axis_size("scan")
    n_det = lax.axis_size("det")
    latent_rows = strip // 4 + 2
    latent_lanes = (width // 4) * f2
    hidden_lanes = (width // 2) * f1
    x = patterns.reshape(cols * strip, width)

    down = [(i, i + 1) for i in range(n_det - 1)]
    up = [(i + 1, i) for i in range(n_det - 1)]
    last, first = lax.optimization_barrier(
        (patterns[0, :, strip - ABOVE :].transpose(1, 0, 2), patterns[0, :, :BELOW].transpose(1, 0, 2))
    )
    above = lax.ppermute(last, "det", down)
    below = lax.ppermute(first, "det", up)
    chips = [(i, i + 1) for i in range(1, n_scan - 1, 2)]
    cores = [(i, i + 1) for i in range(0, n_scan, 2)]
    far_x = swapped(x, "scan", chips)
    halo = jnp.concatenate([above, below], axis=0)
    far_halo = swapped(halo, "scan", chips)

    def cost(flops, moved):
        return pl.CostEstimate(flops=flops, transcendentals=0, bytes_accessed=moved)

    weights = (
        encoder_one,
        encoder_two,
        real_space,
        decoder_one.transpose(0, 1, 3, 2),
        decoder_two.transpose(0, 1, 3, 2),
    )
    w1, w2, wm, wd1, wd2 = pl.pallas_call(
        weights_body,
        in_specs=[pl.BlockSpec(memory_space=pltpu.HBM)] * len(weights),
        out_shape=[
            jax.ShapeDtypeStruct((2 * LANES, hidden_lanes), BF16),
            jax.ShapeDtypeStruct((14 * LANES, 256), BF16),
            jax.ShapeDtypeStruct((4 * LANES, 4 * LANES), BF16),
            jax.ShapeDtypeStruct((6 * LANES, 2 * LANES), BF16),
            jax.ShapeDtypeStruct((4 * hidden_lanes, 2 * LANES), BF16),
        ],
        scratch_shapes=[pltpu.VMEM(w.shape, F32) for w in weights]
        + [pltpu.SemaphoreType.DMA((len(weights),))],
        compiler_params=pltpu.CompilerParams(vmem_limit_bytes=16 << 20),
        cost_estimate=cost(10**9, 4 << 20),
        name="weights",
    )(*[pltpu.with_memory_space_constraint(w, pltpu.HBM) for w in weights])

    n_latent = latent_rows * cols
    n_hidden = (2 * latent_rows + 1) * cols

    def encode(strip_x, strip_halo):
        return pl.pallas_call(
            functools.partial(encode_body, strip=strip, cols=cols, step=f1),
            out_shape=jax.ShapeDtypeStruct((n_latent, latent_lanes), F32),
            scratch_shapes=[pltpu.VMEM((n_hidden, LANES), F32)] * 3
            + [pltpu.VMEM((n_hidden, hidden_lanes), BF16)] * 2
            + [pltpu.VMEM((n_latent, hidden_lanes // 2 + LANES), BF16)] * 2,
            compiler_params=pltpu.CompilerParams(vmem_limit_bytes=ENCODE_VMEM),
            cost_estimate=cost(2 * n_latent * 27 * LANES * latent_lanes * 8, 8 << 20),
            name="encode",
        )(strip_x, strip_halo, w1, w2)

    own = encode(x, halo)
    sibling = swapped(own, "scan", cores)
    other = encode(far_x, far_halo)
    rebuilt, part = pl.pallas_call(
        functools.partial(decode_body, strip=strip, cols=cols),
        out_shape=[
            jax.ShapeDtypeStruct((cols * strip, width), F32),
            jax.ShapeDtypeStruct((1, cols), F32),
        ],
        scratch_shapes=[
            pltpu.VMEM((n_latent, latent_lanes + 2 * LANES), F32),
            pltpu.VMEM(((strip // 2 + 2) * cols, hidden_lanes), BF16),
            pltpu.VMEM(((strip // 2 + 2) * cols, hidden_lanes), BF16),
        ],
        compiler_params=pltpu.CompilerParams(vmem_limit_bytes=DECODE_VMEM),
        cost_estimate=cost(2 * n_latent * 45 * LANES * latent_lanes, 16 << 20),
        name="decode",
    )(own, sibling, other, x, wm, wd1, wd2)
    if n_det == 4:
        misfit = part
        for turn in range(1, n_det):
            misfit = misfit + lax.ppermute(part, "det", [(i, (i + turn) % n_det) for i in range(n_det)])
    else:
        misfit = lax.psum(part, "det")
    return rebuilt.reshape(patterns.shape), misfit


def solution(mesh):
    return jax.shard_map(
        on_device,
        mesh=mesh,
        in_specs=(P("scan", None, "det", None), P(), P(), P(), P(), P()),
        out_specs=(P("scan", None, "det", None), P("scan", None)),
        check_vma=False,
    )
```

```python
import functools

import jax
import jax.numpy as jnp
from jax import lax
from jax.experimental import pallas as pl
from jax.experimental.pallas import tpu as pltpu
from jax.sharding import PartitionSpec as P

ABOVE = 7
BELOW = 4
LANES = 128
F32 = jnp.float32
BF16 = jnp.bfloat16
ENCODE_VMEM = 28 << 20
DECODE_VMEM = 36 << 20


def silu(v):
    return (0.5 * v) * (1.0 + jnp.tanh(0.5 * v))


def split(v):
    high = v.astype(BF16)
    low = (v - high.astype(F32)).astype(BF16)
    return high, low


def iota(shape, dim):
    return lax.broadcasted_iota(jnp.int32, shape, dim)


def spread(values, width):
    k = values.shape[1]
    pick = (iota((k, width), 1) % k == iota((k, width), 0)).astype(F32)
    return jnp.dot(values, pick, precision=lax.Precision.HIGHEST, preferred_element_type=F32)


def put(ref, start, value, lanes=None):
    high, low = split(value)
    half = ref.shape[0] // 2
    rows = value.shape[0]
    lanes = slice(None) if lanes is None else lanes
    ref[start : start + rows, lanes] = high
    ref[half + start : half + start + rows, lanes] = low


def thrice(ref):
    half = ref.shape[0] // 2
    return jnp.concatenate([ref[:half], ref[:half], ref[half:]], axis=0)


def stack(block, times):
    return jnp.concatenate([block] * times, axis=0)


def mosaic(refs):
    return jnp.concatenate([refs[a, b] for a in range(3) for b in range(3)], axis=0)


TAPS = 42
ROW_TAPS = {(0, 0): (0, 1), (1, 0): (2,), (0, 1): (0,), (1, 1): (1, 2)}


def own_lane(shape):
    return iota(shape, len(shape) - 1) ^ (lax.axis_index("scan") % 2 * (LANES // 2))


def loaded(sources, targets, sems):
    copies = [pltpu.make_async_copy(a, b, sems.at[i]) for i, (a, b) in enumerate(zip(sources, targets))]
    for copy in copies:
        copy.start()
    for copy in copies:
        copy.wait()
    return targets


def encoder_weights_body(e1, e2, w1, w2, t1, t2, sems):
    encoder_weights(*loaded((e1, e2), (t1, t2), sems), w1, w2)


def decoder_weights_body(rs, d1, d2, after, wm, wd1, wd2, t1, t2, t3, sems):
    decoder_weights(*loaded((rs, d1, d2), (t1, t2, t3), sems), wm, wd1, wd2)


def encoder_weights(e1, e2, w1, w2):
    f1 = e1.shape[3]
    f2 = e2.shape[3]
    wide = spread(mosaic(e1), w1.shape[1])
    shape = (LANES, w1.shape[1])
    k = iota(shape, 0)
    n = iota(shape, 1)
    group = n // 256
    place = (k - 32 * group + 1) & (LANES - 1)
    a = (place >= TAPS).astype(jnp.int32) + (place >= 2 * TAPS).astype(jnp.int32)
    col = place - TAPS * a
    b = col - 2 * ((n // f1) % (256 // f1))
    good = (b >= 0) & (b <= 2) & ((group > 0) | (col > 0))
    key = jnp.where(good, 3 * a + b, -1)
    value = jnp.zeros(shape, F32)
    for tap in range(9):
        value = jnp.where(key == tap, wide[tap : tap + 1, :], value)
    put(w1, 0, value)
    wide = spread(mosaic(e2), w2.shape[1])
    shape = (256, w2.shape[1])
    out_col = own_lane(shape) // f2
    delta = iota(shape, 0) // f1 - 2 * out_col + 1
    for a in range(3):
        value = jnp.zeros(shape, F32)
        for b in range(3):
            tap = wide[(3 * a + b) * f1 : (3 * a + b + 1) * f1]
            value = jnp.where(delta == b, stack(tap, shape[0] // f1), value)
        put(w2, a * shape[0], value)
    shape = (LANES, w2.shape[1])
    slot = iota(shape, 0) // f1
    value = jnp.zeros(shape, F32)
    for a, at in enumerate((LANES // f1 - 1, 0, 1)):
        tap = stack(wide[3 * a * f1 : (3 * a + 1) * f1], LANES // f1)
        value = jnp.where((slot == at) & (own_lane(shape) // f2 == 0), tap, value)
    put(w2, 3 * 256, value)


def decoder_weights(rs, d1, d2, wm, wd1, wd2):
    f2, f1 = d1.shape[3], d1.shape[2]
    odd = lax.axis_index("scan") % 2
    shape = (LANES, LANES)
    wide = spread(mosaic(rs), LANES)

    def tap(a, b):
        return stack(wide[(3 * a + b) * f2 : (3 * a + b + 1) * f2], LANES // f2)

    def outer(first, b):
        return jnp.where(odd == first, tap(0, b), tap(2, b))

    k = iota(shape, 0) ^ (odd * (LANES // 2))
    n = own_lane(shape)
    same = (k // f2) % 2 == (n // f2) % 2
    for half in range(2):
        row_here = k // (LANES // 2) == half
        col_here = n // (LANES // 2) == half
        for part in range(2):
            if part == 0:
                block = [jnp.where(row_here, tap(1, b), outer(1, b)) for b in range(3)]
                good = same
            else:
                block = [outer(0, b) for b in range(3)]
                good = same & row_here
            sides = jnp.where(good, jnp.where(col_here, block[0], block[2]), 0.0)
            centre = jnp.where(good & col_here, block[1], 0.0)
            put(wm, part * LANES, sides, slice(half * 256, half * 256 + LANES))
            put(wm, part * LANES, centre, slice(half * 256 + LANES, half * 256 + 256))
    per = LANES // f2
    wide = spread(jnp.concatenate([d1[a, b].T for a in range(3) for b in range(3)], axis=0), LANES)
    tap = {(a, b): wide[(3 * a + b) * f2 : (3 * a + b + 1) * f2] for a in range(3) for b in range(3)}
    w_local = iota(shape, 1) // f1
    for p in range(2):
        lanes = slice(p * LANES, (p + 1) * LANES)
        wide_edge = jnp.zeros(shape, F32)
        for r in range(2):
            value = jnp.zeros(shape, F32)
            for b in range(3):
                block = stack(sum(tap[a, b] for a in ROW_TAPS[r, p]), per)
                col = (w_local + b + 1) // 2 - 1
                value = value + jnp.where(col == k // f2, block, 0.0)
                if r == 0:
                    edge = jnp.where(k // f2 == per - 1, -1, jnp.where(k // f2 == 0, per, -9))
                else:
                    edge = jnp.where(k // f2 == 1, -1, jnp.where(k // f2 == 2, per, -9))
                wide_edge = wide_edge + jnp.where(col == edge, block, 0.0)
            put(wd1, r * LANES, value, lanes)
        put(wd1, 2 * LANES, wide_edge, lanes)
    depth = wd2.shape[0] // 4
    shape = (depth, LANES)
    diagonal = iota((f1, f1), 0) == iota((f1, f1), 1)
    column = {
        (a, b): jnp.sum(jnp.where(diagonal, d2[a, b], 0.0), axis=1, keepdims=True)
        for a in range(3)
        for b in range(3)
    }
    for p in range(2):
        for r in range(2):
            value = jnp.zeros(shape, F32)
            for b in range(3):
                block = jnp.broadcast_to(sum(column[a, b] for a in ROW_TAPS[r, p]), (f1, LANES))
                col = (iota(shape, 1) + b + 1) // 2 - 1
                value = value + jnp.where(col == iota(shape, 0) // f1, stack(block, depth // f1), 0.0)
            put(wd2, r * depth, value, slice(p * LANES, (p + 1) * LANES))


def run_starts(runs, cols):
    starts, at = [], 0
    for first, count in runs:
        starts.append((at, at + (count + 1) * cols))
        at += (2 * count + 1) * cols
    return starts, at


def encode_rows(x, halo, w1, w2, out, scratch, runs, strip, cols, step):
    tap0, tap1, tap2, high_map, low_map, high_edge, low_edge = scratch
    starts, total = run_starts(runs, cols)
    n = sum(count for _, count in runs) * cols
    det = lax.axis_index("det")
    not_first = (det > 0).astype(F32)
    not_last = (det < lax.axis_size("det") - 1).astype(F32)
    for (first, count), (even, odd) in zip(runs, starts):
        for e in range(4 * first, 4 * (first + count) + 3):
            if e < ABOVE:
                value = halo[e] * not_first
            elif e < ABOVE + strip:
                value = x[pl.ds(e - ABOVE, cols, stride=strip), :]
            else:
                value = halo[e - strip] * not_last
            rolled = pltpu.roll(value, (TAPS if e % 2 else 2 * TAPS), 1)
            for tap, ref in enumerate((tap0, tap1, tap2)):
                if (e - tap) % 2:
                    continue
                h = (e - tap) // 2 - 2 * first
                if 0 <= h <= 2 * count:
                    start = (odd if h % 2 else even) + (h // 2) * cols
                    ref[start : start + cols, :] = rolled if tap else value
    for ref in (high_edge, low_edge):
        ref[:, :LANES] = jnp.zeros((n, LANES), BF16)
    lane = iota((total, LANES), 1)
    edge_lane = iota((n, LANES), 1)
    groups = high_map.shape[1] // 256

    def taps_of(source):
        taps = ([], [], [])
        for (_, count), (even, odd) in zip(runs, starts):
            for tap, start in zip(taps, (even, odd, even + cols)):
                tap.append(source(start, start + count * cols))
        return [tap[0] if len(tap) == 1 else jnp.concatenate(tap, axis=0) for tap in taps]

    def first_layer(g, carry):
        lanes = pl.ds(pl.multiple_of(g * 256, 256), 256)
        at = (lane - 32 * g + 1) & (LANES - 1)
        packed = jnp.where(at < TAPS, tap0[...], jnp.where(at < 2 * TAPS, tap1[...], tap2[...]))
        high, low = split(packed)
        left = jnp.concatenate([high, low, high], axis=1)
        value = silu(jnp.dot(left, thrice(w1.at[:, lanes]), preferred_element_type=F32))
        high, low = split(value)
        high_map[:, lanes] = high
        low_map[:, lanes] = low
        zero, one, two = taps_of(lambda start, stop: value[start:stop, LANES:])
        one = pltpu.roll(one, step, 1)
        two = pltpu.roll(two, 2 * step, 1)
        edge = jnp.where(edge_lane < step, one, jnp.where(edge_lane < 2 * step, two, zero))
        high, low = split(edge)
        target = pl.ds(pl.multiple_of((g + 1) * LANES, LANES), LANES)
        high_edge[:, target] = high
        low_edge[:, target] = low
        return carry

    lax.fori_loop(0, groups, first_layer, 0)

    def second_layer(g, carry):
        source = pl.ds(pl.multiple_of(g * 256, 256), 256)
        beside = pl.ds(pl.multiple_of(g * LANES, LANES), LANES)
        high = taps_of(lambda start, stop: high_map[start:stop, source]) + [high_edge[:, beside]]
        low = taps_of(lambda start, stop: low_map[start:stop, source]) + [low_edge[:, beside]]
        left = jnp.concatenate(high + low + high, axis=1)
        value = silu(jnp.dot(left, thrice(w2), preferred_element_type=F32))
        done = 0
        for first, count in runs:
            row = first * cols if out.shape[0] > n else done
            out[row : row + count * cols, source] = value[done : done + count * cols]
            done += count * cols
        return carry

    lax.fori_loop(0, groups, second_layer, 0)


def inner_body(x, w1, w2, out, *scratch, **sizes):
    encode_rows(x, None, w1, w2, out, scratch, **sizes)


def border_body(x, halo, w1, w2, inner, out, *scratch, runs, cols, **sizes):
    start = runs[0][1] * cols
    out[start : start + inner.shape[0], :] = inner[...]
    encode_rows(x, halo, w1, w2, out, scratch, runs=runs, cols=cols, **sizes)


def other_body(x, halo, w1, w2, after, out, *scratch, **sizes):
    scan = lax.axis_index("scan")
    inside = (scan > 0) & (scan < lax.axis_size("scan") - 1)

    @pl.when(inside)
    def _():
        encode_rows(x, halo, w1, w2, out, scratch, **sizes)

    @pl.when(jnp.logical_not(inside))
    def _():
        out[...] = jnp.zeros(out.shape, F32)


def decode_body(own, sibling, other, x, wm, wd1, wd2, rebuilt, part, mixed, dh, dl, *, strip, cols):
    n = own.shape[0]
    blocks = own.shape[1] // LANES
    rows = n // cols
    det = lax.axis_index("det")
    not_first = (det > 0).astype(F32)
    not_last = (det < lax.axis_size("det") - 1).astype(F32)
    mixed[:, :LANES] = jnp.zeros((n, LANES), F32)
    mixed[:, (blocks + 1) * LANES :] = jnp.zeros((n, LANES), F32)
    position = iota((n, LANES), 0) % cols
    below = own_lane((n, LANES)) < LANES // 2

    def mix(q, carry):
        lanes = pl.ds(pl.multiple_of(q * LANES, LANES), LANES)
        mine, beside = own[:, lanes], sibling[:, lanes]
        other_high, other_low = split(other[:, lanes])
        sides, centres = [], []
        for half, joined in enumerate((jnp.where(below, mine, beside), jnp.where(below, beside, mine))):
            high, low = split(joined)
            left = jnp.concatenate([high, other_high, low, other_low, high, other_high], axis=1)
            y = jnp.dot(left, thrice(wm.at[:, half * 256 : half * 256 + 256]), preferred_element_type=F32)
            sides.append(y[:, :LANES])
            centres.append(y[:, LANES:])
        before = pltpu.roll(jnp.where(below, sides[0], sides[1]), 1, 0)
        after = pltpu.roll(pltpu.roll(jnp.where(below, sides[1], sides[0]), LANES // 2, 1), n - 1, 0)
        before = jnp.where(position == 0, 0.0, before)
        after = jnp.where(position == cols - 1, 0.0, after)
        value = mine + silu(centres[0] + centres[1] + before + after)
        target = pl.ds(pl.multiple_of((q + 1) * LANES, LANES), LANES)
        mixed[: n - cols, target] = value[: n - cols]
        mixed[n - cols :, target] = value[n - cols :] * not_last
        return carry

    lax.fori_loop(0, blocks, mix, 0)
    count = n - cols
    lane = own_lane((count, LANES))
    middle = (lane >= 32) & (lane < 96)
    outer = own_lane((n, LANES)) >= 96

    def first(q, carry):
        here = pl.ds(pl.multiple_of((q + 1) * LANES, LANES), LANES)
        before = pl.ds(pl.multiple_of(q * LANES, LANES), LANES)
        after = pl.ds(pl.multiple_of((q + 2) * LANES, LANES), LANES)
        high, low = split(mixed[:, here])
        edges = jnp.where(outer, mixed[:, before], mixed[:, after])
        edges = jnp.where(middle, pltpu.roll(edges[cols:], 64, 1), edges[:count])
        edge_high, edge_low = split(edges)
        highs = [high[:count], high[cols:], edge_high]
        lows = [low[:count], low[cols:], edge_low]
        left = jnp.concatenate(highs + lows + highs, axis=1)
        value = silu(jnp.dot(left, thrice(wd1), preferred_element_type=F32))
        target = pl.ds(pl.multiple_of(q * LANES, LANES), LANES)
        for i in range(rows - 1):
            for p in range(2):
                block = value[i * cols : (i + 1) * cols, p * LANES : (p + 1) * LANES]
                if i == 0 and p == 0:
                    block = block * not_first
                if i == rows - 2 and p == 1:
                    block = block * not_last
                high, low = split(block)
                start = (2 * i + p) * cols
                dh[start : start + cols, target] = high
                dl[start : start + cols, target] = low
        return carry

    lax.fori_loop(0, blocks, first, 0)
    total = jnp.zeros((cols, LANES), F32)
    pairs = strip // 2 + 1
    step = 6
    for begin in range(0, pairs, step):
        size = min(step, pairs - begin)
        top = slice(begin * cols, (begin + size) * cols)
        bottom = slice((begin + 1) * cols, (begin + size + 1) * cols)
        high = [dh[top], dh[bottom]]
        low = [dl[top], dl[bottom]]
        left = jnp.concatenate(high + low + high, axis=1)
        value = jnp.dot(left, thrice(wd2), preferred_element_type=F32)
        for i in range(size):
            for p in range(2):
                row = 2 * (begin + i) - 1 + p
                if 0 <= row < strip:
                    block = value[i * cols : (i + 1) * cols, p * LANES : (p + 1) * LANES]
                    where = pl.ds(row, cols, stride=strip)
                    rebuilt[where, :] = block
                    error = block - x[where, :]
                    total = total + error * error
    part[...] = jnp.sum(total.T, axis=0, keepdims=True) * (1.0 / (LANES * LANES))


def far_route(n_scan, n_det):
    route = []
    for i in range(n_scan):
        for j in range(n_det):
            rim = i == 0 or i == n_scan - 1
            to = (i, (j + n_det // 2) % n_det) if rim else (i + 1 if i % 2 else i - 1, j)
            route.append((i * n_det + j, to[0] * n_det + to[1]))
    return route


def on_device(patterns, encoder_one, encoder_two, real_space, decoder_one, decoder_two):
    _, cols, strip, width = patterns.shape
    f1 = encoder_one.shape[3]
    f2 = encoder_two.shape[3]
    n_det = lax.axis_size("det")
    latent_rows = strip // 4 + 2
    latent_lanes = (width // 4) * f2
    hidden_lanes = (width // 2) * f1
    x = patterns.reshape(cols * strip, width)

    down = [(i, (i + 1) % n_det) for i in range(n_det)]
    up = [(j, i) for i, j in down]
    last, first = lax.optimization_barrier(
        (patterns[0, :, strip - ABOVE :].transpose(1, 0, 2), patterns[0, :, :BELOW].transpose(1, 0, 2))
    )
    above = lax.ppermute(last, "det", down)
    below = lax.ppermute(first, "det", up)
    far = far_route(lax.axis_size("scan"), n_det)
    far_x = lax.ppermute(x, ("scan", "det"), far)
    halo = jnp.concatenate([above, below], axis=0)
    far_halo = lax.ppermute(halo, ("scan", "det"), far)

    def cost(flops, moved):
        return pl.CostEstimate(flops=flops, transcendentals=0, bytes_accessed=moved)

    def build(body, shapes, weights, *after):
        return pl.pallas_call(
            body,
            in_specs=[pl.BlockSpec(memory_space=pltpu.HBM)] * len(weights)
            + [pl.BlockSpec(memory_space=pl.ANY)] * len(after),
            out_shape=[jax.ShapeDtypeStruct(shape, BF16) for shape in shapes],
            scratch_shapes=[pltpu.VMEM(w.shape, F32) for w in weights]
            + [pltpu.SemaphoreType.DMA((len(weights),))],
            compiler_params=pltpu.CompilerParams(vmem_limit_bytes=12 << 20),
            cost_estimate=cost(10**9, 4 << 20),
            name=body.__name__,
        )(*[pltpu.with_memory_space_constraint(w, pltpu.HBM) for w in weights], *after)

    w1, w2 = build(
        encoder_weights_body, [(2 * LANES, hidden_lanes), (14 * LANES, 256)], (encoder_one, encoder_two)
    )

    n_latent = latent_rows * cols

    def encode(body, runs, rows, *operands, wait_for=None):
        n_hidden = run_starts(runs, cols)[1]
        n_run = sum(count for _, count in runs) * cols
        return pl.pallas_call(
            functools.partial(body, runs=runs, strip=strip, cols=cols, step=f1),
            out_shape=jax.ShapeDtypeStruct((rows * cols, latent_lanes), F32),
            in_specs=[pl.BlockSpec(memory_space=pl.ANY if ref is wait_for else None) for ref in operands],
            scratch_shapes=[pltpu.VMEM((n_hidden, LANES), F32)] * 3
            + [pltpu.VMEM((n_hidden, hidden_lanes), BF16)] * 2
            + [pltpu.VMEM((n_run, hidden_lanes // 2 + LANES), BF16)] * 2,
            compiler_params=pltpu.CompilerParams(vmem_limit_bytes=ENCODE_VMEM),
            cost_estimate=cost(2 * n_run * 27 * LANES * latent_lanes * 8, 8 << 20),
            name=body.__name__,
        )(*operands)

    n_inner = latent_rows - 3
    inner = encode(inner_body, [(2, n_inner)], n_inner, x, w1, w2)
    own = encode(border_body, [(0, 2), (latent_rows - 1, 1)], latent_rows, x, halo, w1, w2, inner)
    sibling = lax.ppermute(own, "scan", [(i, i ^ 1) for i in range(lax.axis_size("scan"))])
    wm, wd1, wd2 = build(
        decoder_weights_body,
        [(4 * LANES, 4 * LANES), (6 * LANES, 2 * LANES), (4 * hidden_lanes, 2 * LANES)],
        (real_space, decoder_one.transpose(0, 1, 3, 2), decoder_two.transpose(0, 1, 3, 2)),
        own,
    )
    other = encode(other_body, [(0, latent_rows)], latent_rows, far_x, far_halo, w1, w2, wm, wait_for=wm)
    rebuilt, part = pl.pallas_call(
        functools.partial(decode_body, strip=strip, cols=cols),
        out_shape=[
            jax.ShapeDtypeStruct((cols * strip, width), F32),
            jax.ShapeDtypeStruct((1, cols), F32),
        ],
        scratch_shapes=[
            pltpu.VMEM((n_latent, latent_lanes + 2 * LANES), F32),
            pltpu.VMEM(((strip // 2 + 2) * cols, hidden_lanes), BF16),
            pltpu.VMEM(((strip // 2 + 2) * cols, hidden_lanes), BF16),
        ],
        compiler_params=pltpu.CompilerParams(vmem_limit_bytes=DECODE_VMEM),
        cost_estimate=cost(2 * n_latent * 45 * LANES * latent_lanes, 16 << 20),
        name="decode",
    )(own, sibling, other, x, wm, wd1, wd2)
    if n_det & (n_det - 1) == 0:
        misfit, bit = part, 1
        while bit < n_det:
            misfit = misfit + lax.ppermute(misfit, "det", [(i, i ^ bit) for i in range(n_det)])
            bit *= 2
    else:
        misfit = lax.psum(part, "det")
    return rebuilt.reshape(patterns.shape), misfit


def solution(mesh):
    return jax.shard_map(
        on_device,
        mesh=mesh,
        in_specs=(P("scan", None, "det", None), P(), P(), P(), P(), P()),
        out_specs=(P("scan", None, "det", None), P("scan", None)),
        check_vma=False,
    )
```

```python
import functools

import jax
import jax.numpy as jnp
from jax import lax
from jax.experimental import pallas as pl
from jax.experimental.pallas import tpu as pltpu
from jax.sharding import PartitionSpec as P

ABOVE = 7
BELOW = 4
LANES = 128
F32 = jnp.float32
BF16 = jnp.bfloat16
ENCODE_VMEM = 28 << 20
DECODE_VMEM = 36 << 20


def silu(v):
    return (0.5 * v) * (1.0 + jnp.tanh(0.5 * v))


def split(v):
    high = v.astype(BF16)
    low = (v - high.astype(F32)).astype(BF16)
    return high, low


def iota(shape, dim):
    return lax.broadcasted_iota(jnp.int32, shape, dim)


def spread(values, width):
    k = values.shape[1]
    pick = (iota((k, width), 1) % k == iota((k, width), 0)).astype(F32)
    return jnp.dot(values, pick, precision=lax.Precision.HIGHEST, preferred_element_type=F32)


def put(ref, start, value, lanes=None):
    high, low = split(value)
    half = ref.shape[0] // 2
    rows = value.shape[0]
    lanes = slice(None) if lanes is None else lanes
    ref[start : start + rows, lanes] = high
    ref[half + start : half + start + rows, lanes] = low


def thrice(ref):
    half = ref.shape[0] // 2
    return jnp.concatenate([ref[:half], ref[:half], ref[half:]], axis=0)


def stack(block, times):
    return jnp.concatenate([block] * times, axis=0)


def mosaic(refs):
    return jnp.concatenate([refs[a, b] for a in range(3) for b in range(3)], axis=0)


TAPS = 42
ROW_TAPS = {(0, 0): (0, 1), (1, 0): (2,), (0, 1): (0,), (1, 1): (1, 2)}


def own_lane(shape):
    return iota(shape, len(shape) - 1) ^ (lax.axis_index("scan") % 2 * (LANES // 2))


def encoder_weights_body(e1, e2, w1, w2, t1, t2, sems):
    copies = [pltpu.make_async_copy(a, b, sems.at[i]) for i, (a, b) in enumerate(((e1, t1), (e2, t2)))]
    for copy in copies:
        copy.start()
    for copy in copies:
        copy.wait()
    encoder_weights(t1, t2, w1, w2)


def decoder_weights_body(rs, d1, d2, after, wm, wd1, wd2):
    decoder_weights(rs, d1, d2, wm, wd1, wd2)


def encoder_weights(e1, e2, w1, w2):
    f1 = e1.shape[3]
    f2 = e2.shape[3]
    wide = spread(mosaic(e1), w1.shape[1])
    shape = (LANES, w1.shape[1])
    k = iota(shape, 0)
    n = iota(shape, 1)
    group = n // 256
    place = (k - 32 * group + 1) & (LANES - 1)
    a = (place >= TAPS).astype(jnp.int32) + (place >= 2 * TAPS).astype(jnp.int32)
    col = place - TAPS * a
    b = col - 2 * ((n // f1) % (256 // f1))
    good = (b >= 0) & (b <= 2) & ((group > 0) | (col > 0))
    key = jnp.where(good, 3 * a + b, -1)
    value = jnp.zeros(shape, F32)
    for tap in range(9):
        value = jnp.where(key == tap, wide[tap : tap + 1, :], value)
    put(w1, 0, value)
    wide = spread(mosaic(e2), w2.shape[1])
    shape = (256, w2.shape[1])
    out_col = own_lane(shape) // f2
    delta = iota(shape, 0) // f1 - 2 * out_col + 1
    for a in range(3):
        value = jnp.zeros(shape, F32)
        for b in range(3):
            tap = wide[(3 * a + b) * f1 : (3 * a + b + 1) * f1]
            value = jnp.where(delta == b, stack(tap, shape[0] // f1), value)
        put(w2, a * shape[0], value)
    shape = (LANES, w2.shape[1])
    slot = iota(shape, 0) // f1
    value = jnp.zeros(shape, F32)
    for a, at in enumerate((LANES // f1 - 1, 0, 1)):
        tap = stack(wide[3 * a * f1 : (3 * a + 1) * f1], LANES // f1)
        value = jnp.where((slot == at) & (own_lane(shape) // f2 == 0), tap, value)
    put(w2, 3 * 256, value)


def decoder_weights(rs, d1, d2, wm, wd1, wd2):
    f2, f1 = d1.shape[3], d1.shape[2]
    odd = lax.axis_index("scan") % 2
    shape = (LANES, LANES)
    wide = spread(mosaic(rs), LANES)

    def tap(a, b):
        return stack(wide[(3 * a + b) * f2 : (3 * a + b + 1) * f2], LANES // f2)

    def outer(first, b):
        return jnp.where(odd == first, tap(0, b), tap(2, b))

    k = iota(shape, 0) ^ (odd * (LANES // 2))
    n = own_lane(shape)
    same = (k // f2) % 2 == (n // f2) % 2
    for half in range(2):
        row_here = k // (LANES // 2) == half
        col_here = n // (LANES // 2) == half
        for part in range(2):
            if part == 0:
                block = [jnp.where(row_here, tap(1, b), outer(1, b)) for b in range(3)]
                good = same
            else:
                block = [outer(0, b) for b in range(3)]
                good = same & row_here
            sides = jnp.where(good, jnp.where(col_here, block[0], block[2]), 0.0)
            centre = jnp.where(good & col_here, block[1], 0.0)
            put(wm, part * LANES, sides, slice(half * 256, half * 256 + LANES))
            put(wm, part * LANES, centre, slice(half * 256 + LANES, half * 256 + 256))
    per = LANES // f2
    wide = spread(jnp.concatenate([d1[a, b].T for a in range(3) for b in range(3)], axis=0), LANES)
    tap = {(a, b): wide[(3 * a + b) * f2 : (3 * a + b + 1) * f2] for a in range(3) for b in range(3)}
    w_local = iota(shape, 1) // f1
    for p in range(2):
        lanes = slice(p * LANES, (p + 1) * LANES)
        wide_edge = jnp.zeros(shape, F32)
        for r in range(2):
            value = jnp.zeros(shape, F32)
            for b in range(3):
                block = stack(sum(tap[a, b] for a in ROW_TAPS[r, p]), per)
                col = (w_local + b + 1) // 2 - 1
                value = value + jnp.where(col == k // f2, block, 0.0)
                if r == 0:
                    edge = jnp.where(k // f2 == per - 1, -1, jnp.where(k // f2 == 0, per, -9))
                else:
                    edge = jnp.where(k // f2 == 1, -1, jnp.where(k // f2 == 2, per, -9))
                wide_edge = wide_edge + jnp.where(col == edge, block, 0.0)
            put(wd1, r * LANES, value, lanes)
        put(wd1, 2 * LANES, wide_edge, lanes)
    depth = wd2.shape[0] // 4
    shape = (depth, LANES)
    diagonal = iota((f1, f1), 0) == iota((f1, f1), 1)
    column = {
        (a, b): jnp.sum(jnp.where(diagonal, d2[a, b], 0.0), axis=1, keepdims=True)
        for a in range(3)
        for b in range(3)
    }
    for p in range(2):
        for r in range(2):
            value = jnp.zeros(shape, F32)
            for b in range(3):
                block = jnp.broadcast_to(sum(column[a, b] for a in ROW_TAPS[r, p]), (f1, LANES))
                col = (iota(shape, 1) + b + 1) // 2 - 1
                value = value + jnp.where(col == iota(shape, 0) // f1, stack(block, depth // f1), 0.0)
            put(wd2, r * depth, value, slice(p * LANES, (p + 1) * LANES))


def run_starts(runs, cols):
    starts, at = [], 0
    for first, count in runs:
        starts.append((at, at + (count + 1) * cols))
        at += (2 * count + 1) * cols
    return starts, at


def encode_rows(x, halo, w1, w2, out, scratch, runs, strip, cols, step):
    tap0, tap1, tap2, high_map, low_map, high_edge, low_edge = scratch
    starts, total = run_starts(runs, cols)
    n = sum(count for _, count in runs) * cols
    det = lax.axis_index("det")
    not_first = (det > 0).astype(F32)
    not_last = (det < lax.axis_size("det") - 1).astype(F32)
    for (first, count), (even, odd) in zip(runs, starts):
        for e in range(4 * first, 4 * (first + count) + 3):
            if e < ABOVE:
                value = halo[e] * not_first
            elif e < ABOVE + strip:
                value = x[pl.ds(e - ABOVE, cols, stride=strip), :]
            else:
                value = halo[e - strip] * not_last
            rolled = pltpu.roll(value, (TAPS if e % 2 else 2 * TAPS), 1)
            for tap, ref in enumerate((tap0, tap1, tap2)):
                if (e - tap) % 2:
                    continue
                h = (e - tap) // 2 - 2 * first
                if 0 <= h <= 2 * count:
                    start = (odd if h % 2 else even) + (h // 2) * cols
                    ref[start : start + cols, :] = rolled if tap else value
    for ref in (high_edge, low_edge):
        ref[:, :LANES] = jnp.zeros((n, LANES), BF16)
    lane = iota((total, LANES), 1)
    edge_lane = iota((n, LANES), 1)
    groups = high_map.shape[1] // 256

    def taps_of(source):
        taps = ([], [], [])
        for (_, count), (even, odd) in zip(runs, starts):
            for tap, start in zip(taps, (even, odd, even + cols)):
                tap.append(source(start, start + count * cols))
        return [tap[0] if len(tap) == 1 else jnp.concatenate(tap, axis=0) for tap in taps]

    def first_layer(g, carry):
        lanes = pl.ds(pl.multiple_of(g * 256, 256), 256)
        at = (lane - 32 * g + 1) & (LANES - 1)
        packed = jnp.where(at < TAPS, tap0[...], jnp.where(at < 2 * TAPS, tap1[...], tap2[...]))
        high, low = split(packed)
        left = jnp.concatenate([high, low, high], axis=1)
        value = silu(jnp.dot(left, thrice(w1.at[:, lanes]), preferred_element_type=F32))
        high, low = split(value)
        high_map[:, lanes] = high
        low_map[:, lanes] = low
        zero, one, two = taps_of(lambda start, stop: value[start:stop, LANES:])
        one = pltpu.roll(one, step, 1)
        two = pltpu.roll(two, 2 * step, 1)
        edge = jnp.where(edge_lane < step, one, jnp.where(edge_lane < 2 * step, two, zero))
        high, low = split(edge)
        target = pl.ds(pl.multiple_of((g + 1) * LANES, LANES), LANES)
        high_edge[:, target] = high
        low_edge[:, target] = low
        return carry

    lax.fori_loop(0, groups, first_layer, 0, unroll=True)

    def second_layer(g, carry):
        source = pl.ds(pl.multiple_of(g * 256, 256), 256)
        beside = pl.ds(pl.multiple_of(g * LANES, LANES), LANES)
        high = taps_of(lambda start, stop: high_map[start:stop, source]) + [high_edge[:, beside]]
        low = taps_of(lambda start, stop: low_map[start:stop, source]) + [low_edge[:, beside]]
        left = jnp.concatenate(high + low + high, axis=1)
        value = silu(jnp.dot(left, thrice(w2), preferred_element_type=F32))
        done = 0
        for first, count in runs:
            row = first * cols if out.shape[0] > n else done
            out[row : row + count * cols, source] = value[done : done + count * cols]
            done += count * cols
        return carry

    lax.fori_loop(0, groups, second_layer, 0, unroll=True)


def inner_body(x, w1, w2, out, *scratch, **sizes):
    encode_rows(x, None, w1, w2, out, scratch, **sizes)


def border_body(x, halo, w1, w2, inner, out, *scratch, runs, cols, **sizes):
    start = runs[0][1] * cols
    out[start : start + inner.shape[0], :] = inner[...]
    encode_rows(x, halo, w1, w2, out, scratch, runs=runs, cols=cols, **sizes)


def inside_scan(run, out):
    scan = lax.axis_index("scan")
    inside = (scan > 0) & (scan < lax.axis_size("scan") - 1)
    pl.when(inside)(run)

    @pl.when(jnp.logical_not(inside))
    def _():
        out[...] = jnp.zeros(out.shape, F32)


def far_inner_body(x, w1, w2, after, out, *scratch, **sizes):
    inside_scan(lambda: inner_body(x, w1, w2, out, *scratch, **sizes), out)


def far_border_body(x, halo, w1, w2, inner, out, *scratch, **sizes):
    inside_scan(lambda: border_body(x, halo, w1, w2, inner, out, *scratch, **sizes), out)


def decode_body(own, sibling, other, x, wm, wd1, wd2, rebuilt, part, mixed, dh, dl, *, strip, cols):
    n = own.shape[0]
    blocks = own.shape[1] // LANES
    rows = n // cols
    det = lax.axis_index("det")
    not_first = (det > 0).astype(F32)
    not_last = (det < lax.axis_size("det") - 1).astype(F32)
    mixed[:, :LANES] = jnp.zeros((n, LANES), F32)
    mixed[:, (blocks + 1) * LANES :] = jnp.zeros((n, LANES), F32)
    position = iota((n, LANES), 0) % cols
    below = own_lane((n, LANES)) < LANES // 2

    def mix(q, carry):
        lanes = pl.ds(pl.multiple_of(q * LANES, LANES), LANES)
        mine, beside = own[:, lanes], sibling[:, lanes]
        other_high, other_low = split(other[:, lanes])
        sides, centres = [], []
        for half, joined in enumerate((jnp.where(below, mine, beside), jnp.where(below, beside, mine))):
            high, low = split(joined)
            left = jnp.concatenate([high, other_high, low, other_low, high, other_high], axis=1)
            y = jnp.dot(left, thrice(wm.at[:, half * 256 : half * 256 + 256]), preferred_element_type=F32)
            sides.append(y[:, :LANES])
            centres.append(y[:, LANES:])
        before = pltpu.roll(jnp.where(below, sides[0], sides[1]), 1, 0)
        after = pltpu.roll(pltpu.roll(jnp.where(below, sides[1], sides[0]), LANES // 2, 1), n - 1, 0)
        before = jnp.where(position == 0, 0.0, before)
        after = jnp.where(position == cols - 1, 0.0, after)
        value = mine + silu(centres[0] + centres[1] + before + after)
        target = pl.ds(pl.multiple_of((q + 1) * LANES, LANES), LANES)
        mixed[: n - cols, target] = value[: n - cols]
        mixed[n - cols :, target] = value[n - cols :] * not_last
        return carry

    lax.fori_loop(0, blocks, mix, 0, unroll=True)
    count = n - cols
    lane = own_lane((count, LANES))
    middle = (lane >= 32) & (lane < 96)
    outer = own_lane((n, LANES)) >= 96

    def first(q, carry):
        here = pl.ds(pl.multiple_of((q + 1) * LANES, LANES), LANES)
        before = pl.ds(pl.multiple_of(q * LANES, LANES), LANES)
        after = pl.ds(pl.multiple_of((q + 2) * LANES, LANES), LANES)
        high, low = split(mixed[:, here])
        edges = jnp.where(outer, mixed[:, before], mixed[:, after])
        edges = jnp.where(middle, pltpu.roll(edges[cols:], 64, 1), edges[:count])
        edge_high, edge_low = split(edges)
        highs = [high[:count], high[cols:], edge_high]
        lows = [low[:count], low[cols:], edge_low]
        left = jnp.concatenate(highs + lows + highs, axis=1)
        value = silu(jnp.dot(left, thrice(wd1), preferred_element_type=F32))
        target = pl.ds(pl.multiple_of(q * LANES, LANES), LANES)
        for i in range(rows - 1):
            for p in range(2):
                block = value[i * cols : (i + 1) * cols, p * LANES : (p + 1) * LANES]
                if i == 0 and p == 0:
                    block = block * not_first
                if i == rows - 2 and p == 1:
                    block = block * not_last
                high, low = split(block)
                start = (2 * i + p) * cols
                dh[start : start + cols, target] = high
                dl[start : start + cols, target] = low
        return carry

    lax.fori_loop(0, blocks, first, 0, unroll=True)
    total = jnp.zeros((cols, LANES), F32)
    pairs = strip // 2 + 1
    step = 9
    for begin in range(0, pairs, step):
        size = min(step, pairs - begin)
        top = slice(begin * cols, (begin + size) * cols)
        bottom = slice((begin + 1) * cols, (begin + size + 1) * cols)
        high = [dh[top], dh[bottom]]
        low = [dl[top], dl[bottom]]
        left = jnp.concatenate(high + low + high, axis=1)
        value = jnp.dot(left, thrice(wd2), preferred_element_type=F32)
        for i in range(size):
            for p in range(2):
                row = 2 * (begin + i) - 1 + p
                if 0 <= row < strip:
                    block = value[i * cols : (i + 1) * cols, p * LANES : (p + 1) * LANES]
                    where = pl.ds(row, cols, stride=strip)
                    rebuilt[where, :] = block
                    error = block - x[where, :]
                    total = total + error * error
    part[...] = jnp.sum(total.T, axis=0, keepdims=True) * (1.0 / (LANES * LANES))


def far_route(n_scan, n_det):
    route = []
    for i in range(n_scan):
        for j in range(n_det):
            rim = i == 0 or i == n_scan - 1
            to = (i, (j + n_det // 2) % n_det) if rim else (i + 1 if i % 2 else i - 1, j)
            route.append((i * n_det + j, to[0] * n_det + to[1]))
    return route


def on_device(patterns, encoder_one, encoder_two, real_space, decoder_one, decoder_two):
    _, cols, strip, width = patterns.shape
    f1 = encoder_one.shape[3]
    f2 = encoder_two.shape[3]
    n_det = lax.axis_size("det")
    latent_rows = strip // 4 + 2
    latent_lanes = (width // 4) * f2
    hidden_lanes = (width // 2) * f1
    x = patterns.reshape(cols * strip, width)

    down = [(i, (i + 1) % n_det) for i in range(n_det)]
    up = [(j, i) for i, j in down]
    last, first = lax.optimization_barrier(
        (patterns[0, :, strip - ABOVE :].transpose(1, 0, 2), patterns[0, :, :BELOW].transpose(1, 0, 2))
    )
    above = lax.ppermute(last, "det", down)
    below = lax.ppermute(first, "det", up)
    far = far_route(lax.axis_size("scan"), n_det)
    far_x = lax.ppermute(x, ("scan", "det"), far)
    halo = jnp.concatenate([above, below], axis=0)
    far_halo = lax.ppermute(halo, ("scan", "det"), far)

    def cost(flops, moved):
        return pl.CostEstimate(flops=flops, transcendentals=0, bytes_accessed=moved)

    weights = (encoder_one, encoder_two)
    w1, w2 = pl.pallas_call(
        encoder_weights_body,
        in_specs=[pl.BlockSpec(memory_space=pltpu.HBM)] * 2,
        out_shape=[
            jax.ShapeDtypeStruct((2 * LANES, hidden_lanes), BF16),
            jax.ShapeDtypeStruct((14 * LANES, 256), BF16),
        ],
        scratch_shapes=[pltpu.VMEM(w.shape, F32) for w in weights] + [pltpu.SemaphoreType.DMA((2,))],
        compiler_params=pltpu.CompilerParams(vmem_limit_bytes=12 << 20),
        cost_estimate=cost(10**9, 4 << 20),
        name="encoder_weights",
    )(*[pltpu.with_memory_space_constraint(w, pltpu.HBM) for w in weights])

    n_latent = latent_rows * cols

    def encode(body, runs, rows, *operands, wait_for=None):
        n_hidden = run_starts(runs, cols)[1]
        n_run = sum(count for _, count in runs) * cols
        return pl.pallas_call(
            functools.partial(body, runs=runs, strip=strip, cols=cols, step=f1),
            out_shape=jax.ShapeDtypeStruct((rows * cols, latent_lanes), F32),
            in_specs=[pl.BlockSpec(memory_space=pl.ANY if ref is wait_for else None) for ref in operands],
            scratch_shapes=[pltpu.VMEM((n_hidden, LANES), F32)] * 3
            + [pltpu.VMEM((n_hidden, hidden_lanes), BF16)] * 2
            + [pltpu.VMEM((n_run, hidden_lanes // 2 + LANES), BF16)] * 2,
            compiler_params=pltpu.CompilerParams(vmem_limit_bytes=ENCODE_VMEM),
            cost_estimate=cost(2 * n_run * 27 * LANES * latent_lanes * 8, 8 << 20),
            name=body.__name__,
        )(*operands)

    n_inner = latent_rows - 3
    inner_runs, border_runs = [(2, n_inner)], [(0, 2), (latent_rows - 1, 1)]
    inner = encode(inner_body, inner_runs, n_inner, x, w1, w2)
    own = encode(border_body, border_runs, latent_rows, x, halo, w1, w2, inner)
    sibling = lax.ppermute(own, "scan", [(i, i ^ 1) for i in range(lax.axis_size("scan"))])
    wm, wd1, wd2 = pl.pallas_call(
        decoder_weights_body,
        in_specs=[pl.BlockSpec()] * 3 + [pl.BlockSpec(memory_space=pl.ANY)],
        out_shape=[
            jax.ShapeDtypeStruct((4 * LANES, 4 * LANES), BF16),
            jax.ShapeDtypeStruct((6 * LANES, 2 * LANES), BF16),
            jax.ShapeDtypeStruct((4 * hidden_lanes, 2 * LANES), BF16),
        ],
        compiler_params=pltpu.CompilerParams(vmem_limit_bytes=12 << 20),
        cost_estimate=cost(10**9, 4 << 20),
        name="decoder_weights",
    )(real_space, decoder_one.transpose(0, 1, 3, 2), decoder_two.transpose(0, 1, 3, 2), own)
    far_inner = encode(far_inner_body, inner_runs, n_inner, far_x, w1, w2, wm, wait_for=wm)
    other = encode(far_border_body, border_runs, latent_rows, far_x, far_halo, w1, w2, far_inner)
    rebuilt, part = pl.pallas_call(
        functools.partial(decode_body, strip=strip, cols=cols),
        out_shape=[
            jax.ShapeDtypeStruct((cols * strip, width), F32),
            jax.ShapeDtypeStruct((1, cols), F32),
        ],
        scratch_shapes=[
            pltpu.VMEM((n_latent, latent_lanes + 2 * LANES), F32),
            pltpu.VMEM(((strip // 2 + 2) * cols, hidden_lanes), BF16),
            pltpu.VMEM(((strip // 2 + 2) * cols, hidden_lanes), BF16),
        ],
        compiler_params=pltpu.CompilerParams(vmem_limit_bytes=DECODE_VMEM),
        cost_estimate=cost(2 * n_latent * 45 * LANES * latent_lanes, 16 << 20),
        name="decode",
    )(own, sibling, other, x, wm, wd1, wd2)
    if n_det & (n_det - 1) == 0:
        misfit, bit = part, 1
        while bit < n_det:
            misfit = misfit + lax.ppermute(misfit, "det", [(i, i ^ bit) for i in range(n_det)])
            bit *= 2
    else:
        misfit = lax.psum(part, "det")
    return rebuilt.reshape(patterns.shape), misfit


def solution(mesh):
    return jax.shard_map(
        on_device,
        mesh=mesh,
        in_specs=(P("scan", None, "det", None), P(), P(), P(), P(), P()),
        out_specs=(P("scan", None, "det", None), P("scan", None)),
        check_vma=False,
    )
```

```python
import functools

import jax
import jax.numpy as jnp
from jax import lax
from jax.experimental import pallas as pl
from jax.experimental.pallas import tpu as pltpu
from jax.sharding import PartitionSpec as P

ABOVE = 7
BELOW = 4
LANES = 128
F32 = jnp.float32
BF16 = jnp.bfloat16
ENCODE_VMEM = 28 << 20
DECODE_VMEM = 36 << 20


def silu(v):
    return (0.5 * v) * (1.0 + jnp.tanh(0.5 * v))


def split(v):
    high = v.astype(BF16)
    low = (v - high.astype(F32)).astype(BF16)
    return high, low


def iota(shape, dim):
    return lax.broadcasted_iota(jnp.int32, shape, dim)


def spread(values, width):
    k = values.shape[1]
    pick = (iota((k, width), 1) % k == iota((k, width), 0)).astype(F32)
    return jnp.dot(values, pick, precision=lax.Precision.HIGHEST, preferred_element_type=F32)


def put(ref, start, value, lanes=None):
    high, low = split(value)
    half = ref.shape[0] // 2
    rows = value.shape[0]
    lanes = slice(None) if lanes is None else lanes
    ref[start : start + rows, lanes] = high
    ref[half + start : half + start + rows, lanes] = low


def thrice(ref):
    half = ref.shape[0] // 2
    return jnp.concatenate([ref[:half], ref[:half], ref[half:]], axis=0)


def stack(block, times):
    return jnp.concatenate([block] * times, axis=0)


def mosaic(refs):
    return jnp.concatenate([refs[a, b] for a in range(3) for b in range(3)], axis=0)


TAPS = 42
ROW_TAPS = {(0, 0): (0, 1), (1, 0): (2,), (0, 1): (0,), (1, 1): (1, 2)}


def own_lane(shape):
    return iota(shape, len(shape) - 1) ^ (lax.axis_index("scan") % 2 * (LANES // 2))


def edges_body(x, e1, e2, last, first, e1_here, e2_here, bottom, top, sems):
    strip = x.shape[1]
    copies = [
        pltpu.make_async_copy(a, b, sems.at[i])
        for i, (a, b) in enumerate(
            ((x.at[:, strip - 8 :, :], bottom), (x.at[:, :8, :], top), (e1, e1_here), (e2, e2_here))
        )
    ]
    for copy in copies:
        copy.start()
    for copy in copies:
        copy.wait()
    for i in range(ABOVE):
        last[i] = bottom[:, 8 - ABOVE + i, :]
    for i in range(BELOW):
        first[i] = top[:, i, :]


def decoder_weights_body(rs, d1, d2, after, wm, wd1, wd2):
    decoder_weights(rs, d1, d2, wm, wd1, wd2)


def encoder_weights_body(e1, e2, w1, w2):
    f1 = e1.shape[3]
    f2 = e2.shape[3]
    wide = spread(mosaic(e1), w1.shape[1])
    shape = (LANES, w1.shape[1])
    k = iota(shape, 0)
    n = iota(shape, 1)
    group = n // 256
    place = (k - 32 * group + 1) & (LANES - 1)
    a = (place >= TAPS).astype(jnp.int32) + (place >= 2 * TAPS).astype(jnp.int32)
    col = place - TAPS * a
    b = col - 2 * ((n // f1) % (256 // f1))
    good = (b >= 0) & (b <= 2) & ((group > 0) | (col > 0))
    key = jnp.where(good, 3 * a + b, -1)
    value = jnp.zeros(shape, F32)
    for tap in range(9):
        value = jnp.where(key == tap, wide[tap : tap + 1, :], value)
    put(w1, 0, value)
    wide = spread(mosaic(e2), w2.shape[1])
    shape = (256, w2.shape[1])
    out_col = own_lane(shape) // f2
    delta = iota(shape, 0) // f1 - 2 * out_col + 1
    for a in range(3):
        value = jnp.zeros(shape, F32)
        for b in range(3):
            tap = wide[(3 * a + b) * f1 : (3 * a + b + 1) * f1]
            value = jnp.where(delta == b, stack(tap, shape[0] // f1), value)
        put(w2, a * shape[0], value)
    shape = (LANES, w2.shape[1])
    slot = iota(shape, 0) // f1
    value = jnp.zeros(shape, F32)
    for a, at in enumerate((LANES // f1 - 1, 0, 1)):
        tap = stack(wide[3 * a * f1 : (3 * a + 1) * f1], LANES // f1)
        value = jnp.where((slot == at) & (own_lane(shape) // f2 == 0), tap, value)
    put(w2, 3 * 256, value)


def decoder_weights(rs, d1, d2, wm, wd1, wd2):
    f2, f1 = d1.shape[3], d1.shape[2]
    odd = lax.axis_index("scan") % 2
    shape = (LANES, LANES)
    wide = spread(mosaic(rs), LANES)

    def tap(a, b):
        return stack(wide[(3 * a + b) * f2 : (3 * a + b + 1) * f2], LANES // f2)

    def outer(first, b):
        return jnp.where(odd == first, tap(0, b), tap(2, b))

    k = iota(shape, 0) ^ (odd * (LANES // 2))
    n = own_lane(shape)
    same = (k // f2) % 2 == (n // f2) % 2
    for half in range(2):
        row_here = k // (LANES // 2) == half
        col_here = n // (LANES // 2) == half
        for part in range(2):
            if part == 0:
                block = [jnp.where(row_here, tap(1, b), outer(1, b)) for b in range(3)]
                good = same
            else:
                block = [outer(0, b) for b in range(3)]
                good = same & row_here
            sides = jnp.where(good, jnp.where(col_here, block[0], block[2]), 0.0)
            centre = jnp.where(good & col_here, block[1], 0.0)
            put(wm, part * LANES, sides, slice(half * 256, half * 256 + LANES))
            put(wm, part * LANES, centre, slice(half * 256 + LANES, half * 256 + 256))
    per = LANES // f2
    wide = spread(jnp.concatenate([d1[a, b].T for a in range(3) for b in range(3)], axis=0), LANES)
    tap = {(a, b): wide[(3 * a + b) * f2 : (3 * a + b + 1) * f2] for a in range(3) for b in range(3)}
    w_local = iota(shape, 1) // f1
    for p in range(2):
        lanes = slice(p * LANES, (p + 1) * LANES)
        wide_edge = jnp.zeros(shape, F32)
        for r in range(2):
            value = jnp.zeros(shape, F32)
            for b in range(3):
                block = stack(sum(tap[a, b] for a in ROW_TAPS[r, p]), per)
                col = (w_local + b + 1) // 2 - 1
                value = value + jnp.where(col == k // f2, block, 0.0)
                if r == 0:
                    edge = jnp.where(k // f2 == per - 1, -1, jnp.where(k // f2 == 0, per, -9))
                else:
                    edge = jnp.where(k // f2 == 1, -1, jnp.where(k // f2 == 2, per, -9))
                wide_edge = wide_edge + jnp.where(col == edge, block, 0.0)
            put(wd1, r * LANES, value, lanes)
        put(wd1, 2 * LANES, wide_edge, lanes)
    depth = wd2.shape[0] // 4
    shape = (depth, LANES)
    diagonal = iota((f1, f1), 0) == iota((f1, f1), 1)
    column = {
        (a, b): jnp.sum(jnp.where(diagonal, d2[a, b], 0.0), axis=1, keepdims=True)
        for a in range(3)
        for b in range(3)
    }
    for p in range(2):
        for r in range(2):
            value = jnp.zeros(shape, F32)
            for b in range(3):
                block = jnp.broadcast_to(sum(column[a, b] for a in ROW_TAPS[r, p]), (f1, LANES))
                col = (iota(shape, 1) + b + 1) // 2 - 1
                value = value + jnp.where(col == iota(shape, 0) // f1, stack(block, depth // f1), 0.0)
            put(wd2, r * depth, value, slice(p * LANES, (p + 1) * LANES))


def run_starts(runs, cols):
    starts, at = [], 0
    for first, count in runs:
        starts.append((at, at + (count + 1) * cols))
        at += (2 * count + 1) * cols
    return starts, at


def encode_rows(x, halo, w1, w2, out, scratch, runs, strip, cols, step):
    tap0, tap1, tap2, high_map, low_map, high_edge, low_edge = scratch
    starts, total = run_starts(runs, cols)
    n = sum(count for _, count in runs) * cols
    det = lax.axis_index("det")
    not_first = (det > 0).astype(F32)
    not_last = (det < lax.axis_size("det") - 1).astype(F32)
    for (first, count), (even, odd) in zip(runs, starts):
        for e in range(4 * first, 4 * (first + count) + 3):
            if e < ABOVE:
                value = halo[e] * not_first
            elif e < ABOVE + strip:
                value = x[pl.ds(e - ABOVE, cols, stride=strip), :]
            else:
                value = halo[e - strip] * not_last
            rolled = pltpu.roll(value, (TAPS if e % 2 else 2 * TAPS), 1)
            for tap, ref in enumerate((tap0, tap1, tap2)):
                if (e - tap) % 2:
                    continue
                h = (e - tap) // 2 - 2 * first
                if 0 <= h <= 2 * count:
                    start = (odd if h % 2 else even) + (h // 2) * cols
                    ref[start : start + cols, :] = rolled if tap else value
    for ref in (high_edge, low_edge):
        ref[:, :LANES] = jnp.zeros((n, LANES), BF16)
    lane = iota((total, LANES), 1)
    edge_lane = iota((n, LANES), 1)
    groups = high_map.shape[1] // 256

    def taps_of(source):
        taps = ([], [], [])
        for (_, count), (even, odd) in zip(runs, starts):
            for tap, start in zip(taps, (even, odd, even + cols)):
                tap.append(source(start, start + count * cols))
        return [tap[0] if len(tap) == 1 else jnp.concatenate(tap, axis=0) for tap in taps]

    def first_layer(g, carry):
        lanes = pl.ds(pl.multiple_of(g * 256, 256), 256)
        at = (lane - 32 * g + 1) & (LANES - 1)
        packed = jnp.where(at < TAPS, tap0[...], jnp.where(at < 2 * TAPS, tap1[...], tap2[...]))
        high, low = split(packed)
        left = jnp.concatenate([high, low, high], axis=1)
        value = silu(jnp.dot(left, thrice(w1.at[:, lanes]), preferred_element_type=F32))
        high, low = split(value)
        high_map[:, lanes] = high
        low_map[:, lanes] = low
        zero, one, two = taps_of(lambda start, stop: value[start:stop, LANES:])
        one = pltpu.roll(one, step, 1)
        two = pltpu.roll(two, 2 * step, 1)
        edge = jnp.where(edge_lane < step, one, jnp.where(edge_lane < 2 * step, two, zero))
        high, low = split(edge)
        target = pl.ds(pl.multiple_of((g + 1) * LANES, LANES), LANES)
        high_edge[:, target] = high
        low_edge[:, target] = low
        return carry

    lax.fori_loop(0, groups, first_layer, 0, unroll=True)

    def second_layer(g, carry):
        source = pl.ds(pl.multiple_of(g * 256, 256), 256)
        beside = pl.ds(pl.multiple_of(g * LANES, LANES), LANES)
        high = taps_of(lambda start, stop: high_map[start:stop, source]) + [high_edge[:, beside]]
        low = taps_of(lambda start, stop: low_map[start:stop, source]) + [low_edge[:, beside]]
        left = jnp.concatenate(high + low + high, axis=1)
        value = silu(jnp.dot(left, thrice(w2), preferred_element_type=F32))
        done = 0
        for first, count in runs:
            row = first * cols if out.shape[0] > n else done
            out[row : row + count * cols, source] = value[done : done + count * cols]
            done += count * cols
        return carry

    lax.fori_loop(0, groups, second_layer, 0, unroll=True)


def inner_body(x, w1, w2, out, *scratch, **sizes):
    encode_rows(x, None, w1, w2, out, scratch, **sizes)


def own_border_body(x, halo, w1, w2, inner, after, out, *scratch, **sizes):
    border_body(x, halo, w1, w2, inner, out, *scratch, **sizes)


def border_body(x, halo, w1, w2, inner, out, *scratch, runs, cols, **sizes):
    start = runs[0][1] * cols
    out[start : start + inner.shape[0], :] = inner[...]
    encode_rows(x, halo, w1, w2, out, scratch, runs=runs, cols=cols, **sizes)


def inside_scan(run, out):
    scan = lax.axis_index("scan")
    inside = (scan > 0) & (scan < lax.axis_size("scan") - 1)
    pl.when(inside)(run)

    @pl.when(jnp.logical_not(inside))
    def _():
        out[...] = jnp.zeros(out.shape, F32)


def far_inner_body(x, w1, w2, out, *scratch, **sizes):
    inside_scan(lambda: inner_body(x, w1, w2, out, *scratch, **sizes), out)


def far_border_body(x, halo, w1, w2, inner, out, *scratch, **sizes):
    inside_scan(lambda: border_body(x, halo, w1, w2, inner, out, *scratch, **sizes), out)


def decode_body(own, sibling, other, x, wm, wd1, wd2, rebuilt, part, mixed, dh, dl, *, strip, cols):
    n = own.shape[0]
    blocks = own.shape[1] // LANES
    rows = n // cols
    det = lax.axis_index("det")
    not_first = (det > 0).astype(F32)
    not_last = (det < lax.axis_size("det") - 1).astype(F32)
    mixed[:, :LANES] = jnp.zeros((n, LANES), F32)
    mixed[:, (blocks + 1) * LANES :] = jnp.zeros((n, LANES), F32)
    position = iota((n, LANES), 0) % cols
    below = own_lane((n, LANES)) < LANES // 2

    def mix(q, carry):
        lanes = pl.ds(pl.multiple_of(q * LANES, LANES), LANES)
        mine, beside = own[:, lanes], sibling[:, lanes]
        other_high, other_low = split(other[:, lanes])
        sides, centres = [], []
        for half, joined in enumerate((jnp.where(below, mine, beside), jnp.where(below, beside, mine))):
            high, low = split(joined)
            left = jnp.concatenate([high, other_high, low, other_low, high, other_high], axis=1)
            y = jnp.dot(left, thrice(wm.at[:, half * 256 : half * 256 + 256]), preferred_element_type=F32)
            sides.append(y[:, :LANES])
            centres.append(y[:, LANES:])
        before = pltpu.roll(jnp.where(below, sides[0], sides[1]), 1, 0)
        after = pltpu.roll(pltpu.roll(jnp.where(below, sides[1], sides[0]), LANES // 2, 1), n - 1, 0)
        before = jnp.where(position == 0, 0.0, before)
        after = jnp.where(position == cols - 1, 0.0, after)
        value = mine + silu(centres[0] + centres[1] + before + after)
        target = pl.ds(pl.multiple_of((q + 1) * LANES, LANES), LANES)
        mixed[: n - cols, target] = value[: n - cols]
        mixed[n - cols :, target] = value[n - cols :] * not_last
        return carry

    lax.fori_loop(0, blocks, mix, 0, unroll=True)
    count = n - cols
    lane = own_lane((count, LANES))
    middle = (lane >= 32) & (lane < 96)
    outer = own_lane((n, LANES)) >= 96

    def first(q, carry):
        here = pl.ds(pl.multiple_of((q + 1) * LANES, LANES), LANES)
        before = pl.ds(pl.multiple_of(q * LANES, LANES), LANES)
        after = pl.ds(pl.multiple_of((q + 2) * LANES, LANES), LANES)
        high, low = split(mixed[:, here])
        edges = jnp.where(outer, mixed[:, before], mixed[:, after])
        edges = jnp.where(middle, pltpu.roll(edges[cols:], 64, 1), edges[:count])
        edge_high, edge_low = split(edges)
        highs = [high[:count], high[cols:], edge_high]
        lows = [low[:count], low[cols:], edge_low]
        left = jnp.concatenate(highs + lows + highs, axis=1)
        value = silu(jnp.dot(left, thrice(wd1), preferred_element_type=F32))
        target = pl.ds(pl.multiple_of(q * LANES, LANES), LANES)
        for i in range(rows - 1):
            for p in range(2):
                block = value[i * cols : (i + 1) * cols, p * LANES : (p + 1) * LANES]
                if i == 0 and p == 0:
                    block = block * not_first
                if i == rows - 2 and p == 1:
                    block = block * not_last
                high, low = split(block)
                start = (2 * i + p) * cols
                dh[start : start + cols, target] = high
                dl[start : start + cols, target] = low
        return carry

    lax.fori_loop(0, blocks, first, 0, unroll=True)
    total = jnp.zeros((cols, LANES), F32)
    pairs = strip // 2 + 1
    step = 9
    for begin in range(0, pairs, step):
        size = min(step, pairs - begin)
        top = slice(begin * cols, (begin + size) * cols)
        bottom = slice((begin + 1) * cols, (begin + size + 1) * cols)
        high = [dh[top], dh[bottom]]
        low = [dl[top], dl[bottom]]
        left = jnp.concatenate(high + low + high, axis=1)
        value = jnp.dot(left, thrice(wd2), preferred_element_type=F32)
        for i in range(size):
            for p in range(2):
                row = 2 * (begin + i) - 1 + p
                if 0 <= row < strip:
                    block = value[i * cols : (i + 1) * cols, p * LANES : (p + 1) * LANES]
                    where = pl.ds(row, cols, stride=strip)
                    rebuilt[where, :] = block
                    error = block - x[where, :]
                    total = total + error * error
    part[...] = jnp.sum(total.T, axis=0, keepdims=True) * (1.0 / (LANES * LANES))


def far_route(n_scan, n_det, turn):
    route = []
    for i in range(n_scan):
        for j in range(n_det):
            rim = i == 0 or i == n_scan - 1
            to = (i, j ^ turn) if rim else (i + 1 if i % 2 else i - 1, j)
            route.append((i * n_det + j, to[0] * n_det + to[1]))
    return route


def on_device(patterns, encoder_one, encoder_two, real_space, decoder_one, decoder_two):
    _, cols, strip, width = patterns.shape
    f1 = encoder_one.shape[3]
    f2 = encoder_two.shape[3]
    n_det = lax.axis_size("det")
    latent_rows = strip // 4 + 2
    latent_lanes = (width // 4) * f2
    hidden_lanes = (width // 2) * f1
    x = patterns.reshape(cols * strip, width)

    down = [(i, (i + 1) % n_det) for i in range(n_det)]
    up = [(j, i) for i, j in down]
    in_hbm = [
        pltpu.with_memory_space_constraint(a, pltpu.HBM)
        for a in (patterns.reshape(cols, strip, width), encoder_one, encoder_two)
    ]
    last, first, e1, e2 = pl.pallas_call(
        edges_body,
        in_specs=[pl.BlockSpec(memory_space=pltpu.HBM)] * 3,
        out_shape=[
            jax.ShapeDtypeStruct((ABOVE, cols, width), F32),
            jax.ShapeDtypeStruct((BELOW, cols, width), F32),
            jax.ShapeDtypeStruct(encoder_one.shape, F32),
            jax.ShapeDtypeStruct(encoder_two.shape, F32),
        ],
        scratch_shapes=[pltpu.VMEM((cols, 8, width), F32)] * 2 + [pltpu.SemaphoreType.DMA((4,))],
        compiler_params=pltpu.CompilerParams(vmem_limit_bytes=4 << 20),
        name="edges",
    )(*in_hbm)
    above = lax.ppermute(last, "det", down)
    below = lax.ppermute(first, "det", up)
    n_scan = lax.axis_size("scan")
    far_x = lax.ppermute(x, ("scan", "det"), far_route(n_scan, n_det, n_det // 2))
    halo = jnp.concatenate([above, below], axis=0)

    far_halo = lax.ppermute(halo, ("scan", "det"), far_route(n_scan, n_det, 1))

    def cost(flops, moved):
        return pl.CostEstimate(flops=flops, transcendentals=0, bytes_accessed=moved)

    w1, w2 = pl.pallas_call(
        encoder_weights_body,
        out_shape=[
            jax.ShapeDtypeStruct((2 * LANES, hidden_lanes), BF16),
            jax.ShapeDtypeStruct((14 * LANES, 256), BF16),
        ],
        compiler_params=pltpu.CompilerParams(vmem_limit_bytes=12 << 20),
        cost_estimate=cost(2 * 10**9, 0),
        name="encoder_weights",
    )(e1, e2)

    n_latent = latent_rows * cols

    def encode(body, runs, rows, *operands, wait_for=None, weight=0):
        n_hidden = run_starts(runs, cols)[1]
        n_run = sum(count for _, count in runs) * cols
        return pl.pallas_call(
            functools.partial(body, runs=runs, strip=strip, cols=cols, step=f1),
            out_shape=jax.ShapeDtypeStruct((rows * cols, latent_lanes), F32),
            in_specs=[pl.BlockSpec(memory_space=pl.ANY if ref is wait_for else None) for ref in operands],
            scratch_shapes=[pltpu.VMEM((n_hidden, LANES), F32)] * 3
            + [pltpu.VMEM((n_hidden, hidden_lanes), BF16)] * 2
            + [pltpu.VMEM((n_run, hidden_lanes // 2 + LANES), BF16)] * 2,
            compiler_params=pltpu.CompilerParams(vmem_limit_bytes=ENCODE_VMEM),
            cost_estimate=cost(2 * n_run * 27 * LANES * latent_lanes * weight, 0),
            name=body.__name__,
        )(*operands)

    n_inner = latent_rows - 3
    inner_runs, border_runs = [(2, n_inner)], [(0, 2), (latent_rows - 1, 1)]
    inner = encode(inner_body, inner_runs, n_inner, x, w1, w2)
    wm, wd1, wd2 = pl.pallas_call(
        decoder_weights_body,
        in_specs=[pl.BlockSpec()] * 3 + [pl.BlockSpec(memory_space=pl.ANY)],
        out_shape=[
            jax.ShapeDtypeStruct((4 * LANES, 4 * LANES), BF16),
            jax.ShapeDtypeStruct((6 * LANES, 2 * LANES), BF16),
            jax.ShapeDtypeStruct((4 * hidden_lanes, 2 * LANES), BF16),
        ],
        compiler_params=pltpu.CompilerParams(vmem_limit_bytes=12 << 20),
        cost_estimate=cost(0, 0),
        name="decoder_weights",
    )(real_space, decoder_one.transpose(0, 1, 3, 2), decoder_two.transpose(0, 1, 3, 2), inner)
    own = encode(own_border_body, border_runs, latent_rows, x, halo, w1, w2, inner, wm, wait_for=wm)
    sibling = lax.ppermute(own, "scan", [(i, i ^ 1) for i in range(lax.axis_size("scan"))])
    far_inner = encode(far_inner_body, inner_runs, n_inner, far_x, w1, w2, weight=8)
    other = encode(far_border_body, border_runs, latent_rows, far_x, far_halo, w1, w2, far_inner, weight=8)
    rebuilt, part = pl.pallas_call(
        functools.partial(decode_body, strip=strip, cols=cols),
        out_shape=[
            jax.ShapeDtypeStruct((cols * strip, width), F32),
            jax.ShapeDtypeStruct((1, cols), F32),
        ],
        scratch_shapes=[
            pltpu.VMEM((n_latent, latent_lanes + 2 * LANES), F32),
            pltpu.VMEM(((strip // 2 + 2) * cols, hidden_lanes), BF16),
            pltpu.VMEM(((strip // 2 + 2) * cols, hidden_lanes), BF16),
        ],
        compiler_params=pltpu.CompilerParams(vmem_limit_bytes=DECODE_VMEM),
        cost_estimate=cost(2 * n_latent * 45 * LANES * latent_lanes, 16 << 20),
        name="decode",
    )(own, sibling, other, x, wm, wd1, wd2)
    if n_det & (n_det - 1) == 0:
        misfit, bit = part, 1
        while bit < n_det:
            misfit = misfit + lax.ppermute(misfit, "det", [(i, i ^ bit) for i in range(n_det)])
            bit *= 2
    else:
        misfit = lax.psum(part, "det")
    return rebuilt.reshape(patterns.shape), misfit


def solution(mesh):
    return jax.shard_map(
        on_device,
        mesh=mesh,
        in_specs=(P("scan", None, "det", None), P(), P(), P(), P(), P()),
        out_specs=(P("scan", None, "det", None), P("scan", None)),
        check_vma=False,
    )
```

```python
import functools

import jax
import jax.numpy as jnp
from jax import lax
from jax.experimental import pallas as pl
from jax.experimental.pallas import tpu as pltpu
from jax.sharding import PartitionSpec as P

ABOVE = 7
BELOW = 4
LANES = 128
F32 = jnp.float32
BF16 = jnp.bfloat16
ENCODE_VMEM = 28 << 20
DECODE_VMEM = 36 << 20


def silu(v):
    return (0.5 * v) * (1.0 + jnp.tanh(0.5 * v))


def split(v):
    high = v.astype(BF16)
    low = (v - high.astype(F32)).astype(BF16)
    return high, low


def iota(shape, dim):
    return lax.broadcasted_iota(jnp.int32, shape, dim)


def spread(values, width):
    k = values.shape[1]
    pick = (iota((k, width), 1) % k == iota((k, width), 0)).astype(F32)
    return jnp.dot(values, pick, precision=lax.Precision.HIGHEST, preferred_element_type=F32)


def put(ref, start, value, lanes=None):
    high, low = split(value)
    half = ref.shape[0] // 2
    rows = value.shape[0]
    lanes = slice(None) if lanes is None else lanes
    ref[start : start + rows, lanes] = high
    ref[half + start : half + start + rows, lanes] = low


def thrice(ref):
    half = ref.shape[0] // 2
    return jnp.concatenate([ref[:half], ref[:half], ref[half:]], axis=0)


def stack(block, times):
    return jnp.concatenate([block] * times, axis=0)


def mosaic(refs):
    return jnp.concatenate([refs[a, b] for a in range(3) for b in range(3)], axis=0)


TAPS = 42
ROW_TAPS = {(0, 0): (0, 1), (1, 0): (2,), (0, 1): (0,), (1, 1): (1, 2)}


def own_lane(shape):
    return iota(shape, len(shape) - 1) ^ (lax.axis_index("scan") % 2 * (LANES // 2))


def edges_body(x, e1, e2, last, first, e1_here, e2_here, bottom, top, sems):
    strip = x.shape[1]
    copies = [
        pltpu.make_async_copy(a, b, sems.at[i])
        for i, (a, b) in enumerate(
            ((x.at[:, strip - 8 :, :], bottom), (x.at[:, :8, :], top), (e1, e1_here), (e2, e2_here))
        )
    ]
    for copy in copies:
        copy.start()
    for copy in copies:
        copy.wait()
    for i in range(ABOVE):
        last[i] = bottom[:, 8 - ABOVE + i, :]
    for i in range(BELOW):
        first[i] = top[:, i, :]


def decoder_weights_body(rs, d1, d2, after, wm, wd1, wd2):
    decoder_weights(rs, d1, d2, wm, wd1, wd2)


def encoder_weights_body(e1, e2, w1, w2):
    f1 = e1.shape[3]
    f2 = e2.shape[3]
    wide = spread(mosaic(e1), w1.shape[1])
    shape = (LANES, w1.shape[1])
    k = iota(shape, 0)
    n = iota(shape, 1)
    group = n // 256
    place = (k - 32 * group + 1) & (LANES - 1)
    a = (place >= TAPS).astype(jnp.int32) + (place >= 2 * TAPS).astype(jnp.int32)
    col = place - TAPS * a
    b = col - 2 * ((n // f1) % (256 // f1))
    good = (b >= 0) & (b <= 2) & ((group > 0) | (col > 0))
    key = jnp.where(good, 3 * a + b, -1)
    value = jnp.zeros(shape, F32)
    for tap in range(9):
        value = jnp.where(key == tap, wide[tap : tap + 1, :], value)
    put(w1, 0, value)
    wide = spread(mosaic(e2), w2.shape[1])
    shape = (256, w2.shape[1])
    out_col = own_lane(shape) // f2
    delta = iota(shape, 0) // f1 - 2 * out_col + 1
    for a in range(3):
        value = jnp.zeros(shape, F32)
        for b in range(3):
            tap = wide[(3 * a + b) * f1 : (3 * a + b + 1) * f1]
            value = jnp.where(delta == b, stack(tap, shape[0] // f1), value)
        put(w2, a * shape[0], value)
    shape = (LANES, w2.shape[1])
    slot = iota(shape, 0) // f1
    value = jnp.zeros(shape, F32)
    for a, at in enumerate((LANES // f1 - 1, 0, 1)):
        tap = stack(wide[3 * a * f1 : (3 * a + 1) * f1], LANES // f1)
        value = jnp.where((slot == at) & (own_lane(shape) // f2 == 0), tap, value)
    put(w2, 3 * 256, value)


def decoder_weights(rs, d1, d2, wm, wd1, wd2):
    f2, f1 = d1.shape[3], d1.shape[2]
    odd = lax.axis_index("scan") % 2
    shape = (LANES, LANES)
    wide = spread(mosaic(rs), LANES)

    def tap(a, b):
        return stack(wide[(3 * a + b) * f2 : (3 * a + b + 1) * f2], LANES // f2)

    def outer(first, b):
        return jnp.where(odd == first, tap(0, b), tap(2, b))

    k = iota(shape, 0) ^ (odd * (LANES // 2))
    n = own_lane(shape)
    same = (k // f2) % 2 == (n // f2) % 2
    for half in range(2):
        row_here = k // (LANES // 2) == half
        col_here = n // (LANES // 2) == half
        for part in range(2):
            if part == 0:
                block = [jnp.where(row_here, tap(1, b), outer(1, b)) for b in range(3)]
                good = same
            else:
                block = [outer(0, b) for b in range(3)]
                good = same & row_here
            sides = jnp.where(good, jnp.where(col_here, block[0], block[2]), 0.0)
            centre = jnp.where(good & col_here, block[1], 0.0)
            put(wm, part * LANES, sides, slice(half * 256, half * 256 + LANES))
            put(wm, part * LANES, centre, slice(half * 256 + LANES, half * 256 + 256))
    per = LANES // f2
    wide = spread(jnp.concatenate([d1[a, b].T for a in range(3) for b in range(3)], axis=0), LANES)
    tap = {(a, b): wide[(3 * a + b) * f2 : (3 * a + b + 1) * f2] for a in range(3) for b in range(3)}
    w_local = iota(shape, 1) // f1
    for p in range(2):
        lanes = slice(p * LANES, (p + 1) * LANES)
        wide_edge = jnp.zeros(shape, F32)
        for r in range(2):
            value = jnp.zeros(shape, F32)
            for b in range(3):
                block = stack(sum(tap[a, b] for a in ROW_TAPS[r, p]), per)
                col = (w_local + b + 1) // 2 - 1
                value = value + jnp.where(col == k // f2, block, 0.0)
                if r == 0:
                    edge = jnp.where(k // f2 == per - 1, -1, jnp.where(k // f2 == 0, per, -9))
                else:
                    edge = jnp.where(k // f2 == 1, -1, jnp.where(k // f2 == 2, per, -9))
                wide_edge = wide_edge + jnp.where(col == edge, block, 0.0)
            put(wd1, r * LANES, value, lanes)
        put(wd1, 2 * LANES, wide_edge, lanes)
    depth = wd2.shape[0] // 4
    shape = (depth, LANES)
    diagonal = iota((f1, f1), 0) == iota((f1, f1), 1)
    column = {
        (a, b): jnp.sum(jnp.where(diagonal, d2[a, b], 0.0), axis=1, keepdims=True)
        for a in range(3)
        for b in range(3)
    }
    for p in range(2):
        for r in range(2):
            value = jnp.zeros(shape, F32)
            for b in range(3):
                block = jnp.broadcast_to(sum(column[a, b] for a in ROW_TAPS[r, p]), (f1, LANES))
                col = (iota(shape, 1) + b + 1) // 2 - 1
                value = value + jnp.where(col == iota(shape, 0) // f1, stack(block, depth // f1), 0.0)
            put(wd2, r * depth, value, slice(p * LANES, (p + 1) * LANES))


def run_starts(runs, cols):
    starts, at = [], 0
    for first, count in runs:
        starts.append((at, at + (count + 1) * cols))
        at += (2 * count + 1) * cols
    return starts, at


def encode_rows(x, halo, w1, w2, out, scratch, runs, strip, cols, step):
    tap0, tap1, tap2, high_map, low_map, high_edge, low_edge = scratch
    starts, total = run_starts(runs, cols)
    n = sum(count for _, count in runs) * cols
    det = lax.axis_index("det")
    not_first = (det > 0).astype(F32)
    not_last = (det < lax.axis_size("det") - 1).astype(F32)
    for (first, count), (even, odd) in zip(runs, starts):
        for e in range(4 * first, 4 * (first + count) + 3):
            if e < ABOVE:
                value = halo[e] * not_first
            elif e < ABOVE + strip:
                value = x[pl.ds(e - ABOVE, cols, stride=strip), :]
            else:
                value = halo[e - strip] * not_last
            rolled = pltpu.roll(value, (TAPS if e % 2 else 2 * TAPS), 1)
            for tap, ref in enumerate((tap0, tap1, tap2)):
                if (e - tap) % 2:
                    continue
                h = (e - tap) // 2 - 2 * first
                if 0 <= h <= 2 * count:
                    start = (odd if h % 2 else even) + (h // 2) * cols
                    ref[start : start + cols, :] = rolled if tap else value
    for ref in (high_edge, low_edge):
        ref[:, :LANES] = jnp.zeros((n, LANES), BF16)
    lane = iota((total, LANES), 1)
    edge_lane = iota((n, LANES), 1)
    groups = high_map.shape[1] // 256

    def taps_of(source):
        taps = ([], [], [])
        for (_, count), (even, odd) in zip(runs, starts):
            for tap, start in zip(taps, (even, odd, even + cols)):
                tap.append(source(start, start + count * cols))
        return [tap[0] if len(tap) == 1 else jnp.concatenate(tap, axis=0) for tap in taps]

    def first_layer(g, carry):
        lanes = pl.ds(pl.multiple_of(g * 256, 256), 256)
        at = (lane - 32 * g + 1) & (LANES - 1)
        packed = jnp.where(at < TAPS, tap0[...], jnp.where(at < 2 * TAPS, tap1[...], tap2[...]))
        high, low = split(packed)
        left = jnp.concatenate([high, low, high], axis=1)
        value = silu(jnp.dot(left, thrice(w1.at[:, lanes]), preferred_element_type=F32))
        high, low = split(value)
        high_map[:, lanes] = high
        low_map[:, lanes] = low
        zero, one, two = taps_of(lambda start, stop: value[start:stop, LANES:])
        one = pltpu.roll(one, step, 1)
        two = pltpu.roll(two, 2 * step, 1)
        edge = jnp.where(edge_lane < step, one, jnp.where(edge_lane < 2 * step, two, zero))
        high, low = split(edge)
        target = pl.ds(pl.multiple_of((g + 1) * LANES, LANES), LANES)
        high_edge[:, target] = high
        low_edge[:, target] = low
        return carry

    lax.fori_loop(0, groups, first_layer, 0, unroll=True)

    def second_layer(g, carry):
        source = pl.ds(pl.multiple_of(g * 256, 256), 256)
        beside = pl.ds(pl.multiple_of(g * LANES, LANES), LANES)
        high = taps_of(lambda start, stop: high_map[start:stop, source]) + [high_edge[:, beside]]
        low = taps_of(lambda start, stop: low_map[start:stop, source]) + [low_edge[:, beside]]
        left = jnp.concatenate(high + low + high, axis=1)
        value = silu(jnp.dot(left, thrice(w2), preferred_element_type=F32))
        done = 0
        for first, count in runs:
            row = first * cols if out.shape[0] > n else done
            out[row : row + count * cols, source] = value[done : done + count * cols]
            done += count * cols
        return carry

    lax.fori_loop(0, groups, second_layer, 0, unroll=True)


def inner_body(x, w1, w2, out, *scratch, **sizes):
    encode_rows(x, None, w1, w2, out, scratch, **sizes)


def own_border_body(x, halo, w1, w2, inner, after, out, *scratch, **sizes):
    border_body(x, halo, w1, w2, inner, out, *scratch, **sizes)


def border_body(x, halo, w1, w2, inner, out, *scratch, runs, cols, **sizes):
    start = runs[0][1] * cols
    out[start : start + inner.shape[0], :] = inner[...]
    encode_rows(x, halo, w1, w2, out, scratch, runs=runs, cols=cols, **sizes)


def inside_scan(run, out):
    scan = lax.axis_index("scan")
    inside = (scan > 0) & (scan < lax.axis_size("scan") - 1)
    pl.when(inside)(run)

    @pl.when(jnp.logical_not(inside))
    def _():
        out[...] = jnp.zeros(out.shape, F32)


def far_inner_body(x, w1, w2, out, *scratch, **sizes):
    inside_scan(lambda: inner_body(x, w1, w2, out, *scratch, **sizes), out)


def far_border_body(x, halo, w1, w2, inner, out, *scratch, **sizes):
    inside_scan(lambda: border_body(x, halo, w1, w2, inner, out, *scratch, **sizes), out)


def decode_body(own, sibling, other, x, wm, wd1, wd2, rebuilt, part, mixed, dh, dl, *, strip, cols):
    n = own.shape[0]
    blocks = own.shape[1] // LANES
    rows = n // cols
    det = lax.axis_index("det")
    not_first = (det > 0).astype(F32)
    not_last = (det < lax.axis_size("det") - 1).astype(F32)
    mixed[:, :LANES] = jnp.zeros((n, LANES), F32)
    mixed[:, (blocks + 1) * LANES :] = jnp.zeros((n, LANES), F32)
    position = iota((n, LANES), 0) % cols
    below = own_lane((n, LANES)) < LANES // 2

    def mix(q, carry):
        lanes = pl.ds(pl.multiple_of(q * LANES, LANES), LANES)
        mine, beside = own[:, lanes], sibling[:, lanes]
        other_high, other_low = split(other[:, lanes])
        sides, centres = [], []
        for half, joined in enumerate((jnp.where(below, mine, beside), jnp.where(below, beside, mine))):
            high, low = split(joined)
            left = jnp.concatenate([high, other_high, low, other_low, high, other_high], axis=1)
            y = jnp.dot(left, thrice(wm.at[:, half * 256 : half * 256 + 256]), preferred_element_type=F32)
            sides.append(y[:, :LANES])
            centres.append(y[:, LANES:])
        before = pltpu.roll(jnp.where(below, sides[0], sides[1]), 1, 0)
        after = pltpu.roll(pltpu.roll(jnp.where(below, sides[1], sides[0]), LANES // 2, 1), n - 1, 0)
        before = jnp.where(position == 0, 0.0, before)
        after = jnp.where(position == cols - 1, 0.0, after)
        value = mine + silu(centres[0] + centres[1] + before + after)
        target = pl.ds(pl.multiple_of((q + 1) * LANES, LANES), LANES)
        mixed[: n - cols, target] = value[: n - cols]
        mixed[n - cols :, target] = value[n - cols :] * not_last
        return carry

    lax.fori_loop(0, blocks, mix, 0, unroll=True)
    count = n - cols
    lane = own_lane((count, LANES))
    middle = (lane >= 32) & (lane < 96)
    outer = own_lane((n, LANES)) >= 96

    def first(q, carry):
        here = pl.ds(pl.multiple_of((q + 1) * LANES, LANES), LANES)
        before = pl.ds(pl.multiple_of(q * LANES, LANES), LANES)
        after = pl.ds(pl.multiple_of((q + 2) * LANES, LANES), LANES)
        high, low = split(mixed[:, here])
        edges = jnp.where(outer, mixed[:, before], mixed[:, after])
        edges = jnp.where(middle, pltpu.roll(edges[cols:], 64, 1), edges[:count])
        edge_high, edge_low = split(edges)
        highs = [high[:count], high[cols:], edge_high]
        lows = [low[:count], low[cols:], edge_low]
        left = jnp.concatenate(highs + lows + highs, axis=1)
        value = silu(jnp.dot(left, thrice(wd1), preferred_element_type=F32))
        target = pl.ds(pl.multiple_of(q * LANES, LANES), LANES)
        for i in range(rows - 1):
            for p in range(2):
                block = value[i * cols : (i + 1) * cols, p * LANES : (p + 1) * LANES]
                if i == 0 and p == 0:
                    block = block * not_first
                if i == rows - 2 and p == 1:
                    block = block * not_last
                high, low = split(block)
                start = (2 * i + p) * cols
                dh[start : start + cols, target] = high
                dl[start : start + cols, target] = low
        return carry

    lax.fori_loop(0, blocks, first, 0, unroll=True)
    total = jnp.zeros((cols, LANES), F32)
    pairs = strip // 2 + 1
    step = 9
    for begin in range(0, pairs, step):
        size = min(step, pairs - begin)
        top = slice(begin * cols, (begin + size) * cols)
        bottom = slice((begin + 1) * cols, (begin + size + 1) * cols)
        high = [dh[top], dh[bottom]]
        low = [dl[top], dl[bottom]]
        left = jnp.concatenate(high + low + high, axis=1)
        value = jnp.dot(left, thrice(wd2), preferred_element_type=F32)
        for i in range(size):
            for p in range(2):
                row = 2 * (begin + i) - 1 + p
                if 0 <= row < strip:
                    block = value[i * cols : (i + 1) * cols, p * LANES : (p + 1) * LANES]
                    where = pl.ds(row, cols, stride=strip)
                    rebuilt[where, :] = block
                    error = block - x[where, :]
                    total = total + error * error
    part[...] = jnp.sum(total.T, axis=0, keepdims=True) * (1.0 / (LANES * LANES))


def far_route(n_scan, n_det, turn):
    route = []
    for i in range(n_scan):
        for j in range(n_det):
            rim = i == 0 or i == n_scan - 1
            to = (i, j ^ turn) if rim else (i + 1 if i % 2 else i - 1, j)
            route.append((i * n_det + j, to[0] * n_det + to[1]))
    return route


def on_device(patterns, encoder_one, encoder_two, real_space, decoder_one, decoder_two):
    _, cols, strip, width = patterns.shape
    f1 = encoder_one.shape[3]
    f2 = encoder_two.shape[3]
    n_det = lax.axis_size("det")
    latent_rows = strip // 4 + 2
    latent_lanes = (width // 4) * f2
    hidden_lanes = (width // 2) * f1
    x = patterns.reshape(cols * strip, width)

    down = [(i, (i + 1) % n_det) for i in range(n_det)]
    up = [(j, i) for i, j in down]
    in_hbm = [
        pltpu.with_memory_space_constraint(a, pltpu.HBM)
        for a in (patterns.reshape(cols, strip, width), encoder_one, encoder_two)
    ]
    last, first, e1, e2 = pl.pallas_call(
        edges_body,
        in_specs=[pl.BlockSpec(memory_space=pltpu.HBM)] * 3,
        out_shape=[
            jax.ShapeDtypeStruct((ABOVE, cols, width), F32),
            jax.ShapeDtypeStruct((BELOW, cols, width), F32),
            jax.ShapeDtypeStruct(encoder_one.shape, F32),
            jax.ShapeDtypeStruct(encoder_two.shape, F32),
        ],
        scratch_shapes=[pltpu.VMEM((cols, 8, width), F32)] * 2 + [pltpu.SemaphoreType.DMA((4,))],
        compiler_params=pltpu.CompilerParams(vmem_limit_bytes=4 << 20),
        name="edges",
    )(*in_hbm)
    above = lax.ppermute(last, "det", down)
    below = lax.ppermute(first, "det", up)
    n_scan = lax.axis_size("scan")
    far_x = lax.ppermute(x, ("scan", "det"), far_route(n_scan, n_det, n_det // 2))
    halo = jnp.concatenate([above, below], axis=0)

    far_halo = lax.ppermute(halo, ("scan", "det"), far_route(n_scan, n_det, 1))

    def cost(flops, moved):
        return pl.CostEstimate(flops=flops, transcendentals=0, bytes_accessed=moved)

    w1, w2 = pl.pallas_call(
        encoder_weights_body,
        out_shape=[
            jax.ShapeDtypeStruct((2 * LANES, hidden_lanes), BF16),
            jax.ShapeDtypeStruct((14 * LANES, 256), BF16),
        ],
        compiler_params=pltpu.CompilerParams(vmem_limit_bytes=12 << 20),
        cost_estimate=cost(2 * 10**9, 0),
        name="encoder_weights",
    )(e1, e2)

    n_latent = latent_rows * cols

    def encode(body, runs, rows, *operands, wait_for=None, weight=0):
        n_hidden = run_starts(runs, cols)[1]
        n_run = sum(count for _, count in runs) * cols
        return pl.pallas_call(
            functools.partial(body, runs=runs, strip=strip, cols=cols, step=f1),
            out_shape=jax.ShapeDtypeStruct((rows * cols, latent_lanes), F32),
            in_specs=[pl.BlockSpec(memory_space=pl.ANY if ref is wait_for else None) for ref in operands],
            scratch_shapes=[pltpu.VMEM((n_hidden, LANES), F32)] * 3
            + [pltpu.VMEM((n_hidden, hidden_lanes), BF16)] * 2
            + [pltpu.VMEM((n_run, hidden_lanes // 2 + LANES), BF16)] * 2,
            compiler_params=pltpu.CompilerParams(vmem_limit_bytes=ENCODE_VMEM),
            cost_estimate=cost(2 * n_run * 27 * LANES * latent_lanes * weight, 0),
            name=body.__name__,
        )(*operands)

    n_inner = latent_rows - 3
    inner_runs, border_runs = [(2, n_inner)], [(0, 2), (latent_rows - 1, 1)]
    inner = encode(inner_body, inner_runs, n_inner, x, w1, w2)
    wm, wd1, wd2 = pl.pallas_call(
        decoder_weights_body,
        in_specs=[pl.BlockSpec()] * 3 + [pl.BlockSpec(memory_space=pl.ANY)],
        out_shape=[
            jax.ShapeDtypeStruct((4 * LANES, 4 * LANES), BF16),
            jax.ShapeDtypeStruct((6 * LANES, 2 * LANES), BF16),
            jax.ShapeDtypeStruct((4 * hidden_lanes, 2 * LANES), BF16),
        ],
        compiler_params=pltpu.CompilerParams(vmem_limit_bytes=12 << 20),
        cost_estimate=cost(0, 0),
        name="decoder_weights",
    )(real_space, decoder_one.transpose(0, 1, 3, 2), decoder_two.transpose(0, 1, 3, 2), inner)
    own = encode(own_border_body, border_runs, latent_rows, x, halo, w1, w2, inner, wm, wait_for=wm)
    sibling = lax.ppermute(own, "scan", [(i, i ^ 1) for i in range(lax.axis_size("scan"))])
    far_inner = encode(far_inner_body, inner_runs, n_inner, far_x, w1, w2, weight=8)
    other = encode(far_border_body, border_runs, latent_rows, far_x, far_halo, w1, w2, far_inner, weight=8)
    rebuilt, part = pl.pallas_call(
        functools.partial(decode_body, strip=strip, cols=cols),
        out_shape=[
            pltpu.VMEM((cols * strip, width), F32),
            jax.ShapeDtypeStruct((1, cols), F32),
        ],
        scratch_shapes=[
            pltpu.VMEM((n_latent, latent_lanes + 2 * LANES), F32),
            pltpu.VMEM(((strip // 2 + 2) * cols, hidden_lanes), BF16),
            pltpu.VMEM(((strip // 2 + 2) * cols, hidden_lanes), BF16),
        ],
        compiler_params=pltpu.CompilerParams(vmem_limit_bytes=DECODE_VMEM),
        cost_estimate=cost(2 * n_latent * 45 * LANES * latent_lanes, 16 << 20),
        name="decode",
    )(own, sibling, other, x, wm, wd1, wd2)
    if n_det == 4:
        misfit = part
        for bit in (1, 2, 3):
            misfit = misfit + lax.ppermute(part, "det", [(i, i ^ bit) for i in range(n_det)])
    else:
        misfit = lax.psum(part, "det")
    return rebuilt.reshape(patterns.shape), misfit


def solution(mesh):
    return jax.shard_map(
        on_device,
        mesh=mesh,
        in_specs=(P("scan", None, "det", None), P(), P(), P(), P(), P()),
        out_specs=(P("scan", None, "det", None), P("scan", None)),
        check_vma=False,
    )
```

```python
import functools

import jax
import jax.numpy as jnp
from jax import lax
from jax.experimental import pallas as pl
from jax.experimental.pallas import tpu as pltpu
from jax.sharding import PartitionSpec as P

ABOVE = 7
BELOW = 4
LANES = 128
F32 = jnp.float32
BF16 = jnp.bfloat16
ENCODE_VMEM = 28 << 20
DECODE_VMEM = 36 << 20


def silu(v):
    return (0.5 * v) * (1.0 + jnp.tanh(0.5 * v))


def split(v):
    high = v.astype(BF16)
    low = (v - high.astype(F32)).astype(BF16)
    return high, low


def iota(shape, dim):
    return lax.broadcasted_iota(jnp.int32, shape, dim)


def spread(values, width):
    k = values.shape[1]
    pick = (iota((k, width), 1) % k == iota((k, width), 0)).astype(F32)
    return jnp.dot(values, pick, precision=lax.Precision.HIGHEST, preferred_element_type=F32)


def put(ref, start, value, lanes=None):
    high, low = split(value)
    half = ref.shape[0] // 2
    rows = value.shape[0]
    lanes = slice(None) if lanes is None else lanes
    ref[start : start + rows, lanes] = high
    ref[half + start : half + start + rows, lanes] = low


def thrice(ref):
    half = ref.shape[0] // 2
    return jnp.concatenate([ref[:half], ref[:half], ref[half:]], axis=0)


def stack(block, times):
    return jnp.concatenate([block] * times, axis=0)


def mosaic(refs):
    return jnp.concatenate([refs[a, b] for a in range(3) for b in range(3)], axis=0)


TAPS = 42
ROW_TAPS = {(0, 0): (0, 1), (1, 0): (2,), (0, 1): (0,), (1, 1): (1, 2)}


def own_lane(shape):
    return iota(shape, len(shape) - 1) ^ (lax.axis_index("scan") % 2 * (LANES // 2))


def edges_body(x, e1, e2, last, first, e1_here, e2_here, bottom, top, sems):
    strip = x.shape[1]
    copies = [
        pltpu.make_async_copy(a, b, sems.at[i])
        for i, (a, b) in enumerate(
            ((x.at[:, strip - 8 :, :], bottom), (x.at[:, :8, :], top), (e1, e1_here), (e2, e2_here))
        )
    ]
    for copy in copies:
        copy.start()
    for copy in copies:
        copy.wait()
    for i in range(ABOVE):
        last[i] = bottom[:, 8 - ABOVE + i, :]
    for i in range(BELOW):
        first[i] = top[:, i, :]


def decoder_weights_body(rs, d1, d2, after, wm, wd1, wd2):
    decoder_weights(rs, d1, d2, wm, wd1, wd2)


def encoder_weights_body(e1, e2, w1, w2):
    f1 = e1.shape[3]
    f2 = e2.shape[3]
    wide = spread(mosaic(e1), w1.shape[1])
    shape = (LANES, w1.shape[1])
    k = iota(shape, 0)
    n = iota(shape, 1)
    group = n // 256
    place = (k - 32 * group + 1) & (LANES - 1)
    a = (place >= TAPS).astype(jnp.int32) + (place >= 2 * TAPS).astype(jnp.int32)
    col = place - TAPS * a
    b = col - 2 * ((n // f1) % (256 // f1))
    good = (b >= 0) & (b <= 2) & ((group > 0) | (col > 0))
    key = jnp.where(good, 3 * a + b, -1)
    value = jnp.zeros(shape, F32)
    for tap in range(9):
        value = jnp.where(key == tap, wide[tap : tap + 1, :], value)
    put(w1, 0, value)
    wide = spread(mosaic(e2), w2.shape[1])
    shape = (256, w2.shape[1])
    out_col = own_lane(shape) // f2
    delta = iota(shape, 0) // f1 - 2 * out_col + 1
    for a in range(3):
        value = jnp.zeros(shape, F32)
        for b in range(3):
            tap = wide[(3 * a + b) * f1 : (3 * a + b + 1) * f1]
            value = jnp.where(delta == b, stack(tap, shape[0] // f1), value)
        put(w2, a * shape[0], value)
    shape = (LANES, w2.shape[1])
    slot = iota(shape, 0) // f1
    value = jnp.zeros(shape, F32)
    for a, at in enumerate((LANES // f1 - 1, 0, 1)):
        tap = stack(wide[3 * a * f1 : (3 * a + 1) * f1], LANES // f1)
        value = jnp.where((slot == at) & (own_lane(shape) // f2 == 0), tap, value)
    put(w2, 3 * 256, value)


def decoder_weights(rs, d1, d2, wm, wd1, wd2):
    f2, f1 = d1.shape[3], d1.shape[2]
    odd = lax.axis_index("scan") % 2
    shape = (LANES, LANES)
    wide = spread(mosaic(rs), LANES)

    def tap(a, b):
        return stack(wide[(3 * a + b) * f2 : (3 * a + b + 1) * f2], LANES // f2)

    def outer(first, b):
        return jnp.where(odd == first, tap(0, b), tap(2, b))

    k = iota(shape, 0) ^ (odd * (LANES // 2))
    n = own_lane(shape)
    same = (k // f2) % 2 == (n // f2) % 2
    for half in range(2):
        row_here = k // (LANES // 2) == half
        col_here = n // (LANES // 2) == half
        for part in range(2):
            if part == 0:
                block = [jnp.where(row_here, tap(1, b), outer(1, b)) for b in range(3)]
                good = same
            else:
                block = [outer(0, b) for b in range(3)]
                good = same & row_here
            sides = jnp.where(good, jnp.where(col_here, block[0], block[2]), 0.0)
            centre = jnp.where(good & col_here, block[1], 0.0)
            put(wm, part * LANES, sides, slice(half * 256, half * 256 + LANES))
            put(wm, part * LANES, centre, slice(half * 256 + LANES, half * 256 + 256))
    per = LANES // f2
    wide = spread(jnp.concatenate([d1[a, b].T for a in range(3) for b in range(3)], axis=0), LANES)
    tap = {(a, b): wide[(3 * a + b) * f2 : (3 * a + b + 1) * f2] for a in range(3) for b in range(3)}
    w_local = iota(shape, 1) // f1
    for p in range(2):
        lanes = slice(p * LANES, (p + 1) * LANES)
        wide_edge = jnp.zeros(shape, F32)
        for r in range(2):
            value = jnp.zeros(shape, F32)
            for b in range(3):
                block = stack(sum(tap[a, b] for a in ROW_TAPS[r, p]), per)
                col = (w_local + b + 1) // 2 - 1
                value = value + jnp.where(col == k // f2, block, 0.0)
                if r == 0:
                    edge = jnp.where(k // f2 == per - 1, -1, jnp.where(k // f2 == 0, per, -9))
                else:
                    edge = jnp.where(k // f2 == 1, -1, jnp.where(k // f2 == 2, per, -9))
                wide_edge = wide_edge + jnp.where(col == edge, block, 0.0)
            put(wd1, r * LANES, value, lanes)
        put(wd1, 2 * LANES, wide_edge, lanes)
    depth = wd2.shape[0] // 4
    shape = (depth, LANES)
    diagonal = iota((f1, f1), 0) == iota((f1, f1), 1)
    column = {
        (a, b): jnp.sum(jnp.where(diagonal, d2[a, b], 0.0), axis=1, keepdims=True)
        for a in range(3)
        for b in range(3)
    }
    for p in range(2):
        for r in range(2):
            value = jnp.zeros(shape, F32)
            for b in range(3):
                block = jnp.broadcast_to(sum(column[a, b] for a in ROW_TAPS[r, p]), (f1, LANES))
                col = (iota(shape, 1) + b + 1) // 2 - 1
                value = value + jnp.where(col == iota(shape, 0) // f1, stack(block, depth // f1), 0.0)
            put(wd2, r * depth, value, slice(p * LANES, (p + 1) * LANES))


def run_starts(runs, cols):
    starts, at = [], 0
    for first, count in runs:
        starts.append((at, at + (count + 1) * cols))
        at += (2 * count + 1) * cols
    return starts, at


def encode_rows(x, halo, w1, w2, out, scratch, runs, strip, cols, step):
    tap0, tap1, tap2, high_map, low_map, high_edge, low_edge = scratch
    starts, total = run_starts(runs, cols)
    n = sum(count for _, count in runs) * cols
    det = lax.axis_index("det")
    not_first = (det > 0).astype(F32)
    not_last = (det < lax.axis_size("det") - 1).astype(F32)
    for (first, count), (even, odd) in zip(runs, starts):
        for e in range(4 * first, 4 * (first + count) + 3):
            if e < ABOVE:
                value = halo[e] * not_first
            elif e < ABOVE + strip:
                value = x[pl.ds(e - ABOVE, cols, stride=strip), :]
            else:
                value = halo[e - strip] * not_last
            rolled = pltpu.roll(value, (TAPS if e % 2 else 2 * TAPS), 1)
            for tap, ref in enumerate((tap0, tap1, tap2)):
                if (e - tap) % 2:
                    continue
                h = (e - tap) // 2 - 2 * first
                if 0 <= h <= 2 * count:
                    start = (odd if h % 2 else even) + (h // 2) * cols
                    ref[start : start + cols, :] = rolled if tap else value
    for ref in (high_edge, low_edge):
        ref[:, :LANES] = jnp.zeros((n, LANES), BF16)
    lane = iota((total, LANES), 1)
    edge_lane = iota((n, LANES), 1)
    groups = high_map.shape[1] // 256

    def taps_of(source):
        taps = ([], [], [])
        for (_, count), (even, odd) in zip(runs, starts):
            for tap, start in zip(taps, (even, odd, even + cols)):
                tap.append(source(start, start + count * cols))
        return [tap[0] if len(tap) == 1 else jnp.concatenate(tap, axis=0) for tap in taps]

    def first_layer(g, carry):
        lanes = pl.ds(pl.multiple_of(g * 256, 256), 256)
        at = (lane - 32 * g + 1) & (LANES - 1)
        packed = jnp.where(at < TAPS, tap0[...], jnp.where(at < 2 * TAPS, tap1[...], tap2[...]))
        high, low = split(packed)
        left = jnp.concatenate([high, low, high], axis=1)
        value = silu(jnp.dot(left, thrice(w1.at[:, lanes]), preferred_element_type=F32))
        high, low = split(value)
        high_map[:, lanes] = high
        low_map[:, lanes] = low
        zero, one, two = taps_of(lambda start, stop: value[start:stop, LANES:])
        one = pltpu.roll(one, step, 1)
        two = pltpu.roll(two, 2 * step, 1)
        edge = jnp.where(edge_lane < step, one, jnp.where(edge_lane < 2 * step, two, zero))
        high, low = split(edge)
        target = pl.ds(pl.multiple_of((g + 1) * LANES, LANES), LANES)
        high_edge[:, target] = high
        low_edge[:, target] = low
        return carry

    lax.fori_loop(0, groups, first_layer, 0, unroll=True)

    def second_layer(g, carry):
        source = pl.ds(pl.multiple_of(g * 256, 256), 256)
        beside = pl.ds(pl.multiple_of(g * LANES, LANES), LANES)
        high = taps_of(lambda start, stop: high_map[start:stop, source]) + [high_edge[:, beside]]
        low = taps_of(lambda start, stop: low_map[start:stop, source]) + [low_edge[:, beside]]
        left = jnp.concatenate(high + low + high, axis=1)
        value = silu(jnp.dot(left, thrice(w2), preferred_element_type=F32))
        done = 0
        for first, count in runs:
            row = first * cols if out.shape[0] > n else done
            out[row : row + count * cols, source] = value[done : done + count * cols]
            done += count * cols
        return carry

    lax.fori_loop(0, groups, second_layer, 0, unroll=True)


def inner_body(x, w1, w2, out, *scratch, **sizes):
    encode_rows(x, None, w1, w2, out, scratch, **sizes)


def own_border_body(x, halo, w1, w2, inner, after, out, *scratch, **sizes):
    border_body(x, halo, w1, w2, inner, out, *scratch, **sizes)


def border_body(x, halo, w1, w2, inner, out, *scratch, runs, cols, **sizes):
    start = runs[0][1] * cols
    out[start : start + inner.shape[0], :] = inner[...]
    encode_rows(x, halo, w1, w2, out, scratch, runs=runs, cols=cols, **sizes)


def inside_scan(run, out):
    scan = lax.axis_index("scan")
    inside = (scan > 0) & (scan < lax.axis_size("scan") - 1)
    pl.when(inside)(run)

    @pl.when(jnp.logical_not(inside))
    def _():
        out[...] = jnp.zeros(out.shape, F32)


def far_inner_body(x, w1, w2, out, *scratch, **sizes):
    inside_scan(lambda: inner_body(x, w1, w2, out, *scratch, **sizes), out)


def far_border_body(x, halo, w1, w2, inner, out, *scratch, **sizes):
    inside_scan(lambda: border_body(x, halo, w1, w2, inner, out, *scratch, **sizes), out)


def decode_body(own, sibling, other, x, wm, wd1, wd2, rebuilt, part, mixed, dh, dl, *, strip, cols):
    n = own.shape[0]
    blocks = own.shape[1] // LANES
    rows = n // cols
    det = lax.axis_index("det")
    not_first = (det > 0).astype(F32)
    not_last = (det < lax.axis_size("det") - 1).astype(F32)
    mixed[:, :LANES] = jnp.zeros((n, LANES), F32)
    mixed[:, (blocks + 1) * LANES :] = jnp.zeros((n, LANES), F32)
    position = iota((n, LANES), 0) % cols
    below = own_lane((n, LANES)) < LANES // 2

    def mix(q, carry):
        lanes = pl.ds(pl.multiple_of(q * LANES, LANES), LANES)
        mine, beside = own[:, lanes], sibling[:, lanes]
        other_high, other_low = split(other[:, lanes])
        sides, centres = [], []
        for half, joined in enumerate((jnp.where(below, mine, beside), jnp.where(below, beside, mine))):
            high, low = split(joined)
            left = jnp.concatenate([high, other_high, low, other_low, high, other_high], axis=1)
            y = jnp.dot(left, thrice(wm.at[:, half * 256 : half * 256 + 256]), preferred_element_type=F32)
            sides.append(y[:, :LANES])
            centres.append(y[:, LANES:])
        before = pltpu.roll(jnp.where(below, sides[0], sides[1]), 1, 0)
        after = pltpu.roll(pltpu.roll(jnp.where(below, sides[1], sides[0]), LANES // 2, 1), n - 1, 0)
        before = jnp.where(position == 0, 0.0, before)
        after = jnp.where(position == cols - 1, 0.0, after)
        value = mine + silu(centres[0] + centres[1] + before + after)
        target = pl.ds(pl.multiple_of((q + 1) * LANES, LANES), LANES)
        mixed[: n - cols, target] = value[: n - cols]
        mixed[n - cols :, target] = value[n - cols :] * not_last
        return carry

    lax.fori_loop(0, blocks, mix, 0, unroll=True)
    count = n - cols
    lane = own_lane((count, LANES))
    middle = (lane >= 32) & (lane < 96)
    outer = own_lane((n, LANES)) >= 96

    def first(q, carry):
        here = pl.ds(pl.multiple_of((q + 1) * LANES, LANES), LANES)
        before = pl.ds(pl.multiple_of(q * LANES, LANES), LANES)
        after = pl.ds(pl.multiple_of((q + 2) * LANES, LANES), LANES)
        high, low = split(mixed[:, here])
        edges = jnp.where(outer, mixed[:, before], mixed[:, after])
        edges = jnp.where(middle, pltpu.roll(edges[cols:], 64, 1), edges[:count])
        edge_high, edge_low = split(edges)
        highs = [high[:count], high[cols:], edge_high]
        lows = [low[:count], low[cols:], edge_low]
        left = jnp.concatenate(highs + lows + highs, axis=1)
        value = silu(jnp.dot(left, thrice(wd1), preferred_element_type=F32))
        target = pl.ds(pl.multiple_of(q * LANES, LANES), LANES)
        for i in range(rows - 1):
            for p in range(2):
                block = value[i * cols : (i + 1) * cols, p * LANES : (p + 1) * LANES]
                if i == 0 and p == 0:
                    block = block * not_first
                if i == rows - 2 and p == 1:
                    block = block * not_last
                high, low = split(block)
                start = (2 * i + p) * cols
                dh[start : start + cols, target] = high
                dl[start : start + cols, target] = low
        return carry

    lax.fori_loop(0, blocks, first, 0, unroll=True)
    total = jnp.zeros((cols, LANES), F32)
    pairs = strip // 2 + 1
    step = 9
    for begin in range(0, pairs, step):
        size = min(step, pairs - begin)
        top = slice(begin * cols, (begin + size) * cols)
        bottom = slice((begin + 1) * cols, (begin + size + 1) * cols)
        high = [dh[top], dh[bottom]]
        low = [dl[top], dl[bottom]]
        left = jnp.concatenate(high + low + high, axis=1)
        value = jnp.dot(left, thrice(wd2), preferred_element_type=F32)
        for i in range(size):
            for p in range(2):
                row = 2 * (begin + i) - 1 + p
                if 0 <= row < strip:
                    block = value[i * cols : (i + 1) * cols, p * LANES : (p + 1) * LANES]
                    where = pl.ds(row, cols, stride=strip)
                    rebuilt[row * cols : (row + 1) * cols, :] = block
                    error = block - x[where, :]
                    total = total + error * error
    part[...] = jnp.sum(total.T, axis=0, keepdims=True) * (1.0 / (LANES * LANES))


def far_route(n_scan, n_det, turn):
    route = []
    for i in range(n_scan):
        for j in range(n_det):
            rim = i == 0 or i == n_scan - 1
            to = (i, j ^ turn) if rim else (i + 1 if i % 2 else i - 1, j)
            route.append((i * n_det + j, to[0] * n_det + to[1]))
    return route


def on_device(patterns, encoder_one, encoder_two, real_space, decoder_one, decoder_two):
    _, cols, strip, width = patterns.shape
    f1 = encoder_one.shape[3]
    f2 = encoder_two.shape[3]
    n_det = lax.axis_size("det")
    latent_rows = strip // 4 + 2
    latent_lanes = (width // 4) * f2
    hidden_lanes = (width // 2) * f1
    x = patterns.reshape(cols * strip, width)

    down = [(i, (i + 1) % n_det) for i in range(n_det)]
    up = [(j, i) for i, j in down]
    in_hbm = [
        pltpu.with_memory_space_constraint(a, pltpu.HBM)
        for a in (patterns.reshape(cols, strip, width), encoder_one, encoder_two)
    ]
    last, first, e1, e2 = pl.pallas_call(
        edges_body,
        in_specs=[pl.BlockSpec(memory_space=pltpu.HBM)] * 3,
        out_shape=[
            jax.ShapeDtypeStruct((ABOVE, cols, width), F32),
            jax.ShapeDtypeStruct((BELOW, cols, width), F32),
            jax.ShapeDtypeStruct(encoder_one.shape, F32),
            jax.ShapeDtypeStruct(encoder_two.shape, F32),
        ],
        scratch_shapes=[pltpu.VMEM((cols, 8, width), F32)] * 2 + [pltpu.SemaphoreType.DMA((4,))],
        compiler_params=pltpu.CompilerParams(vmem_limit_bytes=4 << 20),
        name="edges",
    )(*in_hbm)
    above = lax.ppermute(last, "det", down)
    below = lax.ppermute(first, "det", up)
    n_scan = lax.axis_size("scan")
    far_x = lax.ppermute(x, ("scan", "det"), far_route(n_scan, n_det, n_det // 2))
    halo = jnp.concatenate([above, below], axis=0)

    far_halo = lax.ppermute(halo, ("scan", "det"), far_route(n_scan, n_det, 1))

    def cost(flops, moved):
        return pl.CostEstimate(flops=flops, transcendentals=0, bytes_accessed=moved)

    w1, w2 = pl.pallas_call(
        encoder_weights_body,
        out_shape=[
            jax.ShapeDtypeStruct((2 * LANES, hidden_lanes), BF16),
            jax.ShapeDtypeStruct((14 * LANES, 256), BF16),
        ],
        compiler_params=pltpu.CompilerParams(vmem_limit_bytes=12 << 20),
        cost_estimate=cost(2 * 10**9, 0),
        name="encoder_weights",
    )(e1, e2)

    n_latent = latent_rows * cols

    def encode(body, runs, rows, *operands, wait_for=None, weight=0):
        n_hidden = run_starts(runs, cols)[1]
        n_run = sum(count for _, count in runs) * cols
        return pl.pallas_call(
            functools.partial(body, runs=runs, strip=strip, cols=cols, step=f1),
            out_shape=jax.ShapeDtypeStruct((rows * cols, latent_lanes), F32),
            in_specs=[pl.BlockSpec(memory_space=pl.ANY if ref is wait_for else None) for ref in operands],
            scratch_shapes=[pltpu.VMEM((n_hidden, LANES), F32)] * 3
            + [pltpu.VMEM((n_hidden, hidden_lanes), BF16)] * 2
            + [pltpu.VMEM((n_run, hidden_lanes // 2 + LANES), BF16)] * 2,
            compiler_params=pltpu.CompilerParams(vmem_limit_bytes=ENCODE_VMEM),
            cost_estimate=cost(2 * n_run * 27 * LANES * latent_lanes * weight, 0),
            name=body.__name__,
        )(*operands)

    n_inner = latent_rows - 3
    inner_runs, border_runs = [(2, n_inner)], [(0, 2), (latent_rows - 1, 1)]
    inner = encode(inner_body, inner_runs, n_inner, x, w1, w2)
    wm, wd1, wd2 = pl.pallas_call(
        decoder_weights_body,
        in_specs=[pl.BlockSpec()] * 3 + [pl.BlockSpec(memory_space=pl.ANY)],
        out_shape=[
            jax.ShapeDtypeStruct((4 * LANES, 4 * LANES), BF16),
            jax.ShapeDtypeStruct((6 * LANES, 2 * LANES), BF16),
            jax.ShapeDtypeStruct((4 * hidden_lanes, 2 * LANES), BF16),
        ],
        compiler_params=pltpu.CompilerParams(vmem_limit_bytes=12 << 20),
        cost_estimate=cost(0, 0),
        name="decoder_weights",
    )(real_space, decoder_one.transpose(0, 1, 3, 2), decoder_two.transpose(0, 1, 3, 2), inner)
    own = encode(own_border_body, border_runs, latent_rows, x, halo, w1, w2, inner, wm, wait_for=wm)
    sibling = lax.ppermute(own, "scan", [(i, i ^ 1) for i in range(lax.axis_size("scan"))])
    far_inner = encode(far_inner_body, inner_runs, n_inner, far_x, w1, w2, weight=8)
    other = encode(far_border_body, border_runs, latent_rows, far_x, far_halo, w1, w2, far_inner, weight=8)
    rebuilt, part = pl.pallas_call(
        functools.partial(decode_body, strip=strip, cols=cols),
        out_shape=[
            pltpu.VMEM((cols * strip, width), F32),
            jax.ShapeDtypeStruct((1, cols), F32),
        ],
        scratch_shapes=[
            pltpu.VMEM((n_latent, latent_lanes + 2 * LANES), F32),
            pltpu.VMEM(((strip // 2 + 2) * cols, hidden_lanes), BF16),
            pltpu.VMEM(((strip // 2 + 2) * cols, hidden_lanes), BF16),
        ],
        compiler_params=pltpu.CompilerParams(vmem_limit_bytes=DECODE_VMEM),
        cost_estimate=cost(2 * n_latent * 45 * LANES * latent_lanes, 16 << 20),
        name="decode",
    )(own, sibling, other, x, wm, wd1, wd2)
    if n_det == 4:
        misfit = part
        for bit in (1, 2, 3):
            misfit = misfit + lax.ppermute(part, "det", [(i, i ^ bit) for i in range(n_det)])
    else:
        misfit = lax.psum(part, "det")
    rebuilt = rebuilt.reshape(strip, cols, width).transpose(1, 0, 2)
    return rebuilt.reshape(patterns.shape), misfit


def solution(mesh):
    return jax.shard_map(
        on_device,
        mesh=mesh,
        in_specs=(P("scan", None, "det", None), P(), P(), P(), P(), P()),
        out_specs=(P("scan", None, "det", None), P("scan", None)),
        check_vma=False,
    )
```

```python
import functools

import jax
import jax.numpy as jnp
from jax import lax
from jax.experimental import pallas as pl
from jax.experimental.pallas import tpu as pltpu
from jax.sharding import PartitionSpec as P

ABOVE = 7
BELOW = 4
LANES = 128
F32 = jnp.float32
BF16 = jnp.bfloat16
ENCODE_VMEM = 28 << 20
DECODE_VMEM = 36 << 20


def silu(v):
    return (0.5 * v) * (1.0 + jnp.tanh(0.5 * v))


def split(v):
    high = v.astype(BF16)
    low = (v - high.astype(F32)).astype(BF16)
    return high, low


def iota(shape, dim):
    return lax.broadcasted_iota(jnp.int32, shape, dim)


def spread(values, width):
    k = values.shape[1]
    pick = (iota((k, width), 1) % k == iota((k, width), 0)).astype(F32)
    return jnp.dot(values, pick, precision=lax.Precision.HIGHEST, preferred_element_type=F32)


def put(ref, start, value, lanes=None):
    high, low = split(value)
    half = ref.shape[0] // 2
    rows = value.shape[0]
    lanes = slice(None) if lanes is None else lanes
    ref[start : start + rows, lanes] = high
    ref[half + start : half + start + rows, lanes] = low


def thrice(ref):
    half = ref.shape[0] // 2
    return jnp.concatenate([ref[:half], ref[:half], ref[half:]], axis=0)


def stack(block, times):
    return jnp.concatenate([block] * times, axis=0)


def mosaic(refs):
    return jnp.concatenate([refs[a, b] for a in range(3) for b in range(3)], axis=0)


TAPS = 42
ROW_TAPS = {(0, 0): (0, 1), (1, 0): (2,), (0, 1): (0,), (1, 1): (1, 2)}


def own_lane(shape):
    return iota(shape, len(shape) - 1) ^ (lax.axis_index("scan") % 2 * (LANES // 2))


def edges_body(x, e1, e2, last, first, e1_here, e2_here, bottom, top, sems):
    strip = x.shape[1]
    copies = [
        pltpu.make_async_copy(a, b, sems.at[i])
        for i, (a, b) in enumerate(
            ((x.at[:, strip - 8 :, :], bottom), (x.at[:, :8, :], top), (e1, e1_here), (e2, e2_here))
        )
    ]
    for copy in copies:
        copy.start()
    for copy in copies:
        copy.wait()
    for i in range(ABOVE):
        last[i] = bottom[:, 8 - ABOVE + i, :]
    for i in range(BELOW):
        first[i] = top[:, i, :]


def decoder_weights_body(rs, d1, d2, after, wm, wd1, wd2):
    decoder_weights(rs, d1, d2, wm, wd1, wd2)


def encoder_weights_body(e1, e2, w1, w2):
    f1 = e1.shape[3]
    f2 = e2.shape[3]
    wide = spread(mosaic(e1), w1.shape[1])
    shape = (LANES, w1.shape[1])
    k = iota(shape, 0)
    n = iota(shape, 1)
    group = n // 256
    place = (k - 32 * group + 1) & (LANES - 1)
    a = (place >= TAPS).astype(jnp.int32) + (place >= 2 * TAPS).astype(jnp.int32)
    col = place - TAPS * a
    b = col - 2 * ((n // f1) % (256 // f1))
    good = (b >= 0) & (b <= 2) & ((group > 0) | (col > 0))
    key = jnp.where(good, 3 * a + b, -1)
    value = jnp.zeros(shape, F32)
    for tap in range(9):
        value = jnp.where(key == tap, wide[tap : tap + 1, :], value)
    put(w1, 0, value)
    wide = spread(mosaic(e2), w2.shape[1])
    shape = (256, w2.shape[1])
    out_col = own_lane(shape) // f2
    delta = iota(shape, 0) // f1 - 2 * out_col + 1
    for a in range(3):
        value = jnp.zeros(shape, F32)
        for b in range(3):
            tap = wide[(3 * a + b) * f1 : (3 * a + b + 1) * f1]
            value = jnp.where(delta == b, stack(tap, shape[0] // f1), value)
        put(w2, a * shape[0], value)
    shape = (LANES, w2.shape[1])
    slot = iota(shape, 0) // f1
    value = jnp.zeros(shape, F32)
    for a, at in enumerate((LANES // f1 - 1, 0, 1)):
        tap = stack(wide[3 * a * f1 : (3 * a + 1) * f1], LANES // f1)
        value = jnp.where((slot == at) & (own_lane(shape) // f2 == 0), tap, value)
    put(w2, 3 * 256, value)


def decoder_weights(rs, d1, d2, wm, wd1, wd2):
    f2, f1 = d1.shape[3], d1.shape[2]
    odd = lax.axis_index("scan") % 2
    shape = (LANES, LANES)
    wide = spread(mosaic(rs), LANES)

    def tap(a, b):
        return stack(wide[(3 * a + b) * f2 : (3 * a + b + 1) * f2], LANES // f2)

    def outer(first, b):
        return jnp.where(odd == first, tap(0, b), tap(2, b))

    k = iota(shape, 0) ^ (odd * (LANES // 2))
    n = own_lane(shape)
    same = (k // f2) % 2 == (n // f2) % 2
    for half in range(2):
        row_here = k // (LANES // 2) == half
        col_here = n // (LANES // 2) == half
        for part in range(2):
            if part == 0:
                block = [jnp.where(row_here, tap(1, b), outer(1, b)) for b in range(3)]
                good = same
            else:
                block = [outer(0, b) for b in range(3)]
                good = same & row_here
            sides = jnp.where(good, jnp.where(col_here, block[0], block[2]), 0.0)
            centre = jnp.where(good & col_here, block[1], 0.0)
            put(wm, part * LANES, sides, slice(half * 256, half * 256 + LANES))
            put(wm, part * LANES, centre, slice(half * 256 + LANES, half * 256 + 256))
    per = LANES // f2
    wide = spread(jnp.concatenate([d1[a, b].T for a in range(3) for b in range(3)], axis=0), LANES)
    tap = {(a, b): wide[(3 * a + b) * f2 : (3 * a + b + 1) * f2] for a in range(3) for b in range(3)}
    w_local = iota(shape, 1) // f1
    for p in range(2):
        lanes = slice(p * LANES, (p + 1) * LANES)
        wide_edge = jnp.zeros(shape, F32)
        for r in range(2):
            value = jnp.zeros(shape, F32)
            for b in range(3):
                block = stack(sum(tap[a, b] for a in ROW_TAPS[r, p]), per)
                col = (w_local + b + 1) // 2 - 1
                value = value + jnp.where(col == k // f2, block, 0.0)
                if r == 0:
                    edge = jnp.where(k // f2 == per - 1, -1, jnp.where(k // f2 == 0, per, -9))
                else:
                    edge = jnp.where(k // f2 == 1, -1, jnp.where(k // f2 == 2, per, -9))
                wide_edge = wide_edge + jnp.where(col == edge, block, 0.0)
            put(wd1, r * LANES, value, lanes)
        put(wd1, 2 * LANES, wide_edge, lanes)
    depth = wd2.shape[0] // 4
    shape = (depth, LANES)
    diagonal = iota((f1, f1), 0) == iota((f1, f1), 1)
    column = {
        (a, b): jnp.sum(jnp.where(diagonal, d2[a, b], 0.0), axis=1, keepdims=True)
        for a in range(3)
        for b in range(3)
    }
    for p in range(2):
        for r in range(2):
            value = jnp.zeros(shape, F32)
            for b in range(3):
                block = jnp.broadcast_to(sum(column[a, b] for a in ROW_TAPS[r, p]), (f1, LANES))
                col = (iota(shape, 1) + b + 1) // 2 - 1
                value = value + jnp.where(col == iota(shape, 0) // f1, stack(block, depth // f1), 0.0)
            put(wd2, r * depth, value, slice(p * LANES, (p + 1) * LANES))


def run_starts(runs, cols):
    starts, at = [], 0
    for first, count in runs:
        starts.append((at, at + (count + 1) * cols))
        at += (2 * count + 1) * cols
    return starts, at


def encode_rows(x, halo, w1, w2, out, scratch, runs, strip, cols, step):
    tap0, tap1, tap2, high_map, low_map, high_edge, low_edge = scratch
    starts, total = run_starts(runs, cols)
    n = sum(count for _, count in runs) * cols
    det = lax.axis_index("det")
    not_first = (det > 0).astype(F32)
    not_last = (det < lax.axis_size("det") - 1).astype(F32)
    for (first, count), (even, odd) in zip(runs, starts):
        for e in range(4 * first, 4 * (first + count) + 3):
            if e < ABOVE:
                value = halo[e] * not_first
            elif e < ABOVE + strip:
                value = x[pl.ds(e - ABOVE, cols, stride=strip), :]
            else:
                value = halo[e - strip] * not_last
            rolled = pltpu.roll(value, (TAPS if e % 2 else 2 * TAPS), 1)
            for tap, ref in enumerate((tap0, tap1, tap2)):
                if (e - tap) % 2:
                    continue
                h = (e - tap) // 2 - 2 * first
                if 0 <= h <= 2 * count:
                    start = (odd if h % 2 else even) + (h // 2) * cols
                    ref[start : start + cols, :] = rolled if tap else value
    for ref in (high_edge, low_edge):
        ref[:, :LANES] = jnp.zeros((n, LANES), BF16)
    lane = iota((total, LANES), 1)
    edge_lane = iota((n, LANES), 1)
    groups = high_map.shape[1] // 256

    def taps_of(source):
        taps = ([], [], [])
        for (_, count), (even, odd) in zip(runs, starts):
            for tap, start in zip(taps, (even, odd, even + cols)):
                tap.append(source(start, start + count * cols))
        return [tap[0] if len(tap) == 1 else jnp.concatenate(tap, axis=0) for tap in taps]

    def first_layer(g, carry):
        lanes = pl.ds(pl.multiple_of(g * 256, 256), 256)
        at = (lane - 32 * g + 1) & (LANES - 1)
        packed = jnp.where(at < TAPS, tap0[...], jnp.where(at < 2 * TAPS, tap1[...], tap2[...]))
        high, low = split(packed)
        left = jnp.concatenate([high, low, high], axis=1)
        value = silu(jnp.dot(left, thrice(w1.at[:, lanes]), preferred_element_type=F32))
        high, low = split(value)
        high_map[:, lanes] = high
        low_map[:, lanes] = low
        zero, one, two = taps_of(lambda start, stop: value[start:stop, LANES:])
        one = pltpu.roll(one, step, 1)
        two = pltpu.roll(two, 2 * step, 1)
        edge = jnp.where(edge_lane < step, one, jnp.where(edge_lane < 2 * step, two, zero))
        high, low = split(edge)
        target = pl.ds(pl.multiple_of((g + 1) * LANES, LANES), LANES)
        high_edge[:, target] = high
        low_edge[:, target] = low
        return carry

    lax.fori_loop(0, groups, first_layer, 0, unroll=True)

    def second_layer(g, carry):
        source = pl.ds(pl.multiple_of(g * 256, 256), 256)
        beside = pl.ds(pl.multiple_of(g * LANES, LANES), LANES)
        high = taps_of(lambda start, stop: high_map[start:stop, source]) + [high_edge[:, beside]]
        low = taps_of(lambda start, stop: low_map[start:stop, source]) + [low_edge[:, beside]]
        left = jnp.concatenate(high + low + high, axis=1)
        value = silu(jnp.dot(left, thrice(w2), preferred_element_type=F32))
        done = 0
        for first, count in runs:
            row = first * cols if out.shape[0] > n else done
            out[row : row + count * cols, source] = value[done : done + count * cols]
            done += count * cols
        return carry

    lax.fori_loop(0, groups, second_layer, 0, unroll=True)


def inner_body(x, w1, w2, out, *scratch, **sizes):
    encode_rows(x, None, w1, w2, out, scratch, **sizes)


def own_border_body(x, halo, w1, w2, inner, after, out, *scratch, **sizes):
    border_body(x, halo, w1, w2, inner, out, *scratch, **sizes)


def border_body(x, halo, w1, w2, inner, out, *scratch, runs, cols, **sizes):
    start = runs[0][1] * cols
    out[start : start + inner.shape[0], :] = inner[...]
    encode_rows(x, halo, w1, w2, out, scratch, runs=runs, cols=cols, **sizes)


def inside_scan(run, out):
    scan = lax.axis_index("scan")
    inside = (scan > 0) & (scan < lax.axis_size("scan") - 1)
    pl.when(inside)(run)

    @pl.when(jnp.logical_not(inside))
    def _():
        out[...] = jnp.zeros(out.shape, F32)


def far_inner_body(x, w1, w2, out, *scratch, **sizes):
    inside_scan(lambda: inner_body(x, w1, w2, out, *scratch, **sizes), out)


def far_border_body(x, halo, w1, w2, inner, out, *scratch, **sizes):
    inside_scan(lambda: border_body(x, halo, w1, w2, inner, out, *scratch, **sizes), out)


def decode_body(own, sibling, other, x, wm, wd1, wd2, rebuilt, part, mixed, dh, dl, *, strip, cols):
    n = own.shape[0]
    blocks = own.shape[1] // LANES
    rows = n // cols
    det = lax.axis_index("det")
    not_first = (det > 0).astype(F32)
    not_last = (det < lax.axis_size("det") - 1).astype(F32)
    mixed[:, :LANES] = jnp.zeros((n, LANES), F32)
    mixed[:, (blocks + 1) * LANES :] = jnp.zeros((n, LANES), F32)
    position = iota((n, LANES), 0) % cols
    below = own_lane((n, LANES)) < LANES // 2

    def mix(q, carry):
        lanes = pl.ds(pl.multiple_of(q * LANES, LANES), LANES)
        mine, beside = own[:, lanes], sibling[:, lanes]
        other_high, other_low = split(other[:, lanes])
        sides, centres = [], []
        for half, joined in enumerate((jnp.where(below, mine, beside), jnp.where(below, beside, mine))):
            high, low = split(joined)
            left = jnp.concatenate([high, other_high, low, other_low, high, other_high], axis=1)
            y = jnp.dot(left, thrice(wm.at[:, half * 256 : half * 256 + 256]), preferred_element_type=F32)
            sides.append(y[:, :LANES])
            centres.append(y[:, LANES:])
        before = pltpu.roll(jnp.where(below, sides[0], sides[1]), 1, 0)
        after = pltpu.roll(pltpu.roll(jnp.where(below, sides[1], sides[0]), LANES // 2, 1), n - 1, 0)
        before = jnp.where(position == 0, 0.0, before)
        after = jnp.where(position == cols - 1, 0.0, after)
        value = mine + silu(centres[0] + centres[1] + before + after)
        target = pl.ds(pl.multiple_of((q + 1) * LANES, LANES), LANES)
        mixed[: n - cols, target] = value[: n - cols]
        mixed[n - cols :, target] = value[n - cols :] * not_last
        return carry

    lax.fori_loop(0, blocks, mix, 0, unroll=True)
    count = n - cols
    lane = own_lane((count, LANES))
    middle = (lane >= 32) & (lane < 96)
    outer = own_lane((n, LANES)) >= 96

    def first(q, carry):
        here = pl.ds(pl.multiple_of((q + 1) * LANES, LANES), LANES)
        before = pl.ds(pl.multiple_of(q * LANES, LANES), LANES)
        after = pl.ds(pl.multiple_of((q + 2) * LANES, LANES), LANES)
        high, low = split(mixed[:, here])
        edges = jnp.where(outer, mixed[:, before], mixed[:, after])
        edges = jnp.where(middle, pltpu.roll(edges[cols:], 64, 1), edges[:count])
        edge_high, edge_low = split(edges)
        highs = [high[:count], high[cols:], edge_high]
        lows = [low[:count], low[cols:], edge_low]
        left = jnp.concatenate(highs + lows + highs, axis=1)
        value = silu(jnp.dot(left, thrice(wd1), preferred_element_type=F32))
        target = pl.ds(pl.multiple_of(q * LANES, LANES), LANES)
        for i in range(rows - 1):
            for p in range(2):
                block = value[i * cols : (i + 1) * cols, p * LANES : (p + 1) * LANES]
                if i == 0 and p == 0:
                    block = block * not_first
                if i == rows - 2 and p == 1:
                    block = block * not_last
                high, low = split(block)
                start = (2 * i + p) * cols
                dh[start : start + cols, target] = high
                dl[start : start + cols, target] = low
        return carry

    lax.fori_loop(0, blocks, first, 0, unroll=True)
    total = jnp.zeros((cols, LANES), F32)
    pairs = strip // 2 + 1
    step = 12
    for begin in range(0, pairs, step):
        size = min(step, pairs - begin)
        top = slice(begin * cols, (begin + size) * cols)
        bottom = slice((begin + 1) * cols, (begin + size + 1) * cols)
        high = [dh[top], dh[bottom]]
        low = [dl[top], dl[bottom]]
        left = jnp.concatenate(high + low + high, axis=1)
        value = jnp.dot(left, thrice(wd2), preferred_element_type=F32)
        for i in range(size):
            for p in range(2):
                row = 2 * (begin + i) - 1 + p
                if 0 <= row < strip:
                    block = value[i * cols : (i + 1) * cols, p * LANES : (p + 1) * LANES]
                    where = pl.ds(row, cols, stride=strip)
                    rebuilt[row * cols : (row + 1) * cols, :] = block
                    error = block - x[where, :]
                    total = total + error * error
    part[...] = jnp.sum(total.T, axis=0, keepdims=True) * (1.0 / (LANES * LANES))


def far_route(n_scan, n_det, turn):
    route = []
    for i in range(n_scan):
        for j in range(n_det):
            rim = i == 0 or i == n_scan - 1
            to = (i, j ^ turn) if rim else (i + 1 if i % 2 else i - 1, j)
            route.append((i * n_det + j, to[0] * n_det + to[1]))
    return route


def on_device(patterns, encoder_one, encoder_two, real_space, decoder_one, decoder_two):
    _, cols, strip, width = patterns.shape
    f1 = encoder_one.shape[3]
    f2 = encoder_two.shape[3]
    n_det = lax.axis_size("det")
    latent_rows = strip // 4 + 2
    latent_lanes = (width // 4) * f2
    hidden_lanes = (width // 2) * f1
    x = patterns.reshape(cols * strip, width)

    down = [(i, (i + 1) % n_det) for i in range(n_det)]
    up = [(j, i) for i, j in down]
    in_hbm = [
        pltpu.with_memory_space_constraint(a, pltpu.HBM)
        for a in (patterns.reshape(cols, strip, width), encoder_one, encoder_two)
    ]
    last, first, e1, e2 = pl.pallas_call(
        edges_body,
        in_specs=[pl.BlockSpec(memory_space=pltpu.HBM)] * 3,
        out_shape=[
            jax.ShapeDtypeStruct((ABOVE, cols, width), F32),
            jax.ShapeDtypeStruct((BELOW, cols, width), F32),
            jax.ShapeDtypeStruct(encoder_one.shape, F32),
            jax.ShapeDtypeStruct(encoder_two.shape, F32),
        ],
        scratch_shapes=[pltpu.VMEM((cols, 8, width), F32)] * 2 + [pltpu.SemaphoreType.DMA((4,))],
        compiler_params=pltpu.CompilerParams(vmem_limit_bytes=4 << 20),
        name="edges",
    )(*in_hbm)
    above = lax.ppermute(last, "det", down)
    below = lax.ppermute(first, "det", up)
    n_scan = lax.axis_size("scan")
    far_x = lax.ppermute(x, ("scan", "det"), far_route(n_scan, n_det, n_det // 2))
    halo = jnp.concatenate([above, below], axis=0)

    far_halo = lax.ppermute(halo, ("scan", "det"), far_route(n_scan, n_det, 1))

    def cost(flops, moved):
        return pl.CostEstimate(flops=flops, transcendentals=0, bytes_accessed=moved)

    w1, w2 = pl.pallas_call(
        encoder_weights_body,
        out_shape=[
            jax.ShapeDtypeStruct((2 * LANES, hidden_lanes), BF16),
            jax.ShapeDtypeStruct((14 * LANES, 256), BF16),
        ],
        compiler_params=pltpu.CompilerParams(vmem_limit_bytes=12 << 20),
        cost_estimate=cost(2 * 10**9, 0),
        name="encoder_weights",
    )(e1, e2)

    n_latent = latent_rows * cols

    def encode(body, runs, rows, *operands, wait_for=None, weight=0):
        n_hidden = run_starts(runs, cols)[1]
        n_run = sum(count for _, count in runs) * cols
        return pl.pallas_call(
            functools.partial(body, runs=runs, strip=strip, cols=cols, step=f1),
            out_shape=jax.ShapeDtypeStruct((rows * cols, latent_lanes), F32),
            in_specs=[pl.BlockSpec(memory_space=pl.ANY if ref is wait_for else None) for ref in operands],
            scratch_shapes=[pltpu.VMEM((n_hidden, LANES), F32)] * 3
            + [pltpu.VMEM((n_hidden, hidden_lanes), BF16)] * 2
            + [pltpu.VMEM((n_run, hidden_lanes // 2 + LANES), BF16)] * 2,
            compiler_params=pltpu.CompilerParams(vmem_limit_bytes=ENCODE_VMEM),
            cost_estimate=cost(2 * n_run * 27 * LANES * latent_lanes * weight, 0),
            name=body.__name__,
        )(*operands)

    n_inner = latent_rows - 3
    inner_runs, border_runs = [(2, n_inner)], [(0, 2), (latent_rows - 1, 1)]
    inner = encode(inner_body, inner_runs, n_inner, x, w1, w2)
    wm, wd1, wd2 = pl.pallas_call(
        decoder_weights_body,
        in_specs=[pl.BlockSpec()] * 3 + [pl.BlockSpec(memory_space=pl.ANY)],
        out_shape=[
            jax.ShapeDtypeStruct((4 * LANES, 4 * LANES), BF16),
            jax.ShapeDtypeStruct((6 * LANES, 2 * LANES), BF16),
            jax.ShapeDtypeStruct((4 * hidden_lanes, 2 * LANES), BF16),
        ],
        compiler_params=pltpu.CompilerParams(vmem_limit_bytes=12 << 20),
        cost_estimate=cost(0, 0),
        name="decoder_weights",
    )(real_space, decoder_one.transpose(0, 1, 3, 2), decoder_two.transpose(0, 1, 3, 2), inner)
    own = encode(own_border_body, border_runs, latent_rows, x, halo, w1, w2, inner, wm, wait_for=wm)
    sibling = lax.ppermute(own, "scan", [(i, i ^ 1) for i in range(lax.axis_size("scan"))])
    far_inner = encode(far_inner_body, inner_runs, n_inner, far_x, w1, w2, weight=8)
    other = encode(far_border_body, border_runs, latent_rows, far_x, far_halo, w1, w2, far_inner, weight=8)
    rebuilt, part = pl.pallas_call(
        functools.partial(decode_body, strip=strip, cols=cols),
        out_shape=[
            pltpu.VMEM((cols * strip, width), F32),
            jax.ShapeDtypeStruct((1, cols), F32),
        ],
        scratch_shapes=[
            pltpu.VMEM((n_latent, latent_lanes + 2 * LANES), F32),
            pltpu.VMEM(((strip // 2 + 2) * cols, hidden_lanes), BF16),
            pltpu.VMEM(((strip // 2 + 2) * cols, hidden_lanes), BF16),
        ],
        compiler_params=pltpu.CompilerParams(vmem_limit_bytes=DECODE_VMEM),
        cost_estimate=cost(2 * n_latent * 45 * LANES * latent_lanes, 16 << 20),
        name="decode",
    )(own, sibling, other, x, wm, wd1, wd2)
    if n_det == 4:
        misfit = part
        for bit in (1, 2, 3):
            misfit = misfit + lax.ppermute(part, "det", [(i, i ^ bit) for i in range(n_det)])
    else:
        misfit = lax.psum(part, "det")
    rebuilt = rebuilt.reshape(strip, cols, width).transpose(1, 0, 2)
    return rebuilt.reshape(patterns.shape), misfit


def solution(mesh):
    return jax.shard_map(
        on_device,
        mesh=mesh,
        in_specs=(P("scan", None, "det", None), P(), P(), P(), P(), P()),
        out_specs=(P("scan", None, "det", None), P("scan", None)),
        check_vma=False,
    )
```
